32 devices in a mesh: grp: 4 (over y, x), dev: 8 (over z, core).
Axes of the slice: x: 2, y: 2, z: 4, core: 2. Of those that a mesh axis runs over, the one named last changes fastest.
Arguments:
- positions: bfloat16 [3, 131072], P(None, ('grp', 'dev')), may hold values from 0 to 1.5
- features: bfloat16 [131072, 128], P(('grp', 'dev')), may hold values from -6 to 6
- tile_first: int32 [256], P(('grp', 'dev')), may hold values from 0 to 31
- tile_second: int32 [256], P(('grp', 'dev')), may hold values from 0 to 127
- count_first: int32 [256], P(('grp', 'dev')), may hold values from 32 to 128
- count_second: int32 [256], P(('grp', 'dev')), may hold values from 32 to 128
- w_first: bfloat16 [128, 128], replicated, may hold values from -0.5 to 0.5
- w_second: bfloat16 [128, 128], replicated, may hold values from -0.5 to 0.5
- radial_weight: bfloat16 [16, 128], replicated, may hold values from -3 to 3
- mix_weight: bfloat16 [128, 128], replicated, may hold values from -0.5 to 0.5
- out_weight: float32 [128], replicated, may hold values from -1.5 to 1.5
Outputs:
- forces: float32 [3, 131072], P(None, ('grp', 'dev'))
The draws below stay inside these ranges and needn't reach their ends.
All inputs are finite; a program needn't handle non-finite values.
Results may differ from the reference program's by a relative error of at most 0.0023.
Values may be sent and summed in bfloat16 or wider, within the bound.
No kernel may reach another device: no remote copies, remote signals or barrier semaphores. Data moves between devices by JAX's collectives and lax.ppermute only.
A program may use at most 64 MiB of HBM per device.

```python
import jax
import jax.numpy as jnp
from jax import lax

CELL = 128
CELLS_DEV = 32
TILE_DEV = 8
LAT = 128
NB = 16
BEADS = 131072
TILES = 256
N_GRP = 4
N_DEV = 8


def set_ends(drawn, key, low, high):
    shape = drawn.shape
    place = [jax.random.randint(jax.random.fold_in(key, axis), (), 0, shape[axis]) for axis in range(len(shape))]
    drawn = drawn.at[tuple(place)].set(low)
    longest = shape.index(max(shape))
    place[longest] = (place[longest] + 1) % shape[longest]
    return drawn.at[tuple(place)].set(high)


def steps_of(key, extent, cuts, least, top_value):
    level = 1.0
    for axis_at, blocks in cuts:
        draws = jax.random.uniform(jax.random.fold_in(jax.random.fold_in(key, 6), axis_at), (blocks,), jnp.float32, least / len(cuts), top_value / len(cuts))
        level = level * jnp.repeat(jnp.exp(draws), extent[axis_at] // blocks).reshape((-1,) + (1,) * (len(extent) - 1 - axis_at))
    return level


def bell_draw(key, dims, scale, bound, cuts=(), kind=jnp.bfloat16):
    factor_of = steps_of(key, dims, cuts, -0.22, 0.18) if cuts else 1.0
    result = jax.random.normal(key, dims, jnp.float32) * scale * factor_of
    return jnp.minimum(jnp.maximum(result, -bound), bound).astype(kind)


def setup_inputs(seed: int = 0) -> dict:
    arg_keys = jax.random.split(jax.random.key(seed), 12)
    return {
        "positions": jnp.clip(1.5 * jax.random.uniform(arg_keys[0], (3, BEADS), jnp.float32) ** steps_of(arg_keys[0], (3, BEADS), ((1, 32),), -0.2, 0.2), 0.0, 1.5).astype(jnp.bfloat16),
        "features": bell_draw(arg_keys[1], (BEADS, LAT), 1.0, 6.0, ((0, 32),)),
        "tile_first": set_ends(jax.random.randint(arg_keys[2], (TILES,), 0, CELLS_DEV), jax.random.fold_in(arg_keys[2], 1), 0, CELLS_DEV - 1).astype(jnp.int32),
        "tile_second": set_ends(jax.random.randint(arg_keys[3], (TILES,), 0, 4 * CELLS_DEV), jax.random.fold_in(arg_keys[3], 1), 0, (4 * CELLS_DEV) - 1).astype(jnp.int32),
        "count_first": set_ends(jax.random.randint(arg_keys[4], (TILES,), CELL // 4, CELL + 1), jax.random.fold_in(arg_keys[4], 1), CELL // 4, CELL).astype(jnp.int32),
        "count_second": set_ends(jax.random.randint(arg_keys[5], (TILES,), CELL // 4, CELL + 1), jax.random.fold_in(arg_keys[5], 1), CELL // 4, CELL).astype(jnp.int32),
        "w_first": bell_draw(arg_keys[6], (LAT, LAT), LAT ** -0.5, 0.5),
        "w_second": bell_draw(arg_keys[7], (LAT, LAT), LAT ** -0.5, 0.5),
        "radial_weight": bell_draw(arg_keys[8], (NB, LAT), 4 ** -0.5, 3.0),
        "mix_weight": bell_draw(arg_keys[9], (LAT, LAT), LAT ** -0.5, 0.5),
        "out_weight": bell_draw(arg_keys[10], (LAT,), (LAT // 8) ** -0.5, 1.5, (), jnp.float32),
    }


def project(features, weight):
    return jnp.dot(features, weight, preferred_element_type=jnp.float32).astype(jnp.bfloat16)


def silu_slope(values):
    sigma = jax.nn.sigmoid(values)
    return sigma * (1.0 + values * (1.0 - sigma))


def tile_gradients(first_pos, second_pos, first_proj, second_proj, first_live, second_live, radial_weight, mix_weight, out_weight):
    slots = first_pos.shape[1]
    diff = first_pos[:, :, None] - second_pos[:, None, :]
    dist_sq = jnp.sum(diff * diff, axis=0).reshape(-1)
    centers = jnp.arange(NB, dtype=jnp.float32) * (6.75 / NB)
    offset = dist_sq[None, :] - centers[:, None]
    basis_exact = jnp.exp(-2.0 * offset * offset)
    basis = basis_exact.astype(jnp.bfloat16)
    radial = lax.dot_general(basis, radial_weight, (((0,), (0,)), ((), ())), preferred_element_type=jnp.float32)
    radial = radial.reshape(slots, slots, -1)
    summed = radial + first_proj.astype(jnp.float32)[:, None, :] + second_proj.astype(jnp.float32)[None, :, :]
    summed = summed.reshape(slots * slots, -1)
    latent = jax.nn.silu(summed).astype(jnp.bfloat16)
    pre = jnp.dot(latent, mix_weight, preferred_element_type=jnp.float32)
    readout = jnp.sum(jax.nn.silu(pre) * out_weight[None, :], axis=1)
    weights = (first_live[:, None] * second_live[None, :]).reshape(-1) / slots
    envelope_base = 1.0 - dist_sq / 8.0
    envelope = envelope_base * envelope_base
    d_readout = envelope * weights
    d_pre = (d_readout[:, None] * out_weight[None, :] * silu_slope(pre)).astype(jnp.bfloat16)
    d_latent = lax.dot_general(d_pre, mix_weight, (((1,), (1,)), ((), ())), preferred_element_type=jnp.float32)
    d_summed = (d_latent * silu_slope(summed)).astype(jnp.bfloat16)
    d_basis = lax.dot_general(radial_weight, d_summed, (((1,), (1,)), ((), ())), preferred_element_type=jnp.float32)
    d_dist = jnp.sum(d_basis * basis_exact * (-4.0 * offset), axis=0)
    d_dist = d_dist + readout * weights * 2.0 * envelope_base * (-0.125)
    d_dist = d_dist.reshape(slots, slots)
    pull = 2.0 * diff * d_dist[None, :, :]
    return jnp.sum(pull, axis=2), -jnp.sum(pull, axis=1)


def live_mask(count):
    return (jnp.arange(CELL, dtype=jnp.int32) < count).astype(jnp.float32)


def reference(positions, features, tile_first, tile_second, count_first, count_second, w_first, w_second, radial_weight, mix_weight, out_weight):
    first_all = project(features, w_first)
    second_all = project(features, w_second)
    pos_all = positions.astype(jnp.float32)
    owner = (jnp.arange(TILES, dtype=jnp.int32) // TILE_DEV).astype(jnp.int32)
    group = owner // N_DEV
    member = owner % N_DEV
    block = tile_second // CELLS_DEV
    other = ((group - block // 2) % N_GRP) * N_DEV + (member - block % 2) % N_DEV
    first_cell = (owner * CELLS_DEV + tile_first).astype(jnp.int32)
    second_cell = (other * CELLS_DEV + tile_second % CELLS_DEV).astype(jnp.int32)

    def visit(total, item):
        cell_a, cell_b, num_a, num_b = item
        start_a = (cell_a * CELL).astype(jnp.int32)
        start_b = (cell_b * CELL).astype(jnp.int32)
        pos_a = lax.dynamic_slice_in_dim(pos_all, start_a, CELL, 1)
        pos_b = lax.dynamic_slice_in_dim(pos_all, start_b, CELL, 1)
        proj_a = lax.dynamic_slice_in_dim(first_all, start_a, CELL, 0)
        proj_b = lax.dynamic_slice_in_dim(second_all, start_b, CELL, 0)
        grad_a, grad_b = tile_gradients(pos_a, pos_b, proj_a, proj_b, live_mask(num_a), live_mask(num_b), radial_weight, mix_weight, out_weight)
        total = lax.dynamic_update_slice_in_dim(total, lax.dynamic_slice_in_dim(total, start_a, CELL, 1) + grad_a, start_a, 1)
        total = lax.dynamic_update_slice_in_dim(total, lax.dynamic_slice_in_dim(total, start_b, CELL, 1) + grad_b, start_b, 1)
        return total, None

    start = jnp.zeros((3, BEADS), jnp.float32)
    total, unused = lax.scan(visit, start, (first_cell, second_cell, count_first, count_second))
    return -total
```

```python
import functools

import jax
import jax.numpy as jnp
from jax import lax
from jax.experimental import pallas as pl
from jax.experimental.pallas import tpu as pltpu
from jax.sharding import PartitionSpec as P

CELL = 128
NB = 16
ROWS = 16
PACKED = CELL + 16
EARLY = 2
F32, BF = jnp.float32, jnp.bfloat16
LAST = (((1,), (1,)), ((), ()))
VMEM = pl.BlockSpec(memory_space=pltpu.VMEM)


def shifted(array, groups, members):
    n_grp, n_dev = lax.axis_size("grp"), lax.axis_size("dev")
    if groups == 0:
        return lax.ppermute(array, "dev", [(i, (i + members) % n_dev) for i in range(n_dev)])
    if members == 0:
        return lax.ppermute(array, "grp", [(i, (i + groups) % n_grp) for i in range(n_grp)])
    pairs = [
        (g * n_dev + d, (g + groups) % n_grp * n_dev + (d + members) % n_dev)
        for g in range(n_grp)
        for d in range(n_dev)
    ]
    return lax.ppermute(array, ("grp", "dev"), pairs)


def dot(a, b):
    return jnp.dot(a, b, preferred_element_type=F32)


def cell_at(ref, cell):
    return ref[pl.ds(pl.multiple_of(cell * CELL, CELL), CELL), :]


def place_at(ref, cell):
    return ref[:, pl.ds(pl.multiple_of(cell * CELL, CELL), CELL)]


def tall(places):
    return jnp.concatenate([places.astype(F32), jnp.zeros((5, CELL), F32)], axis=0)


def pack_kernel(wanted, own_f, own_p, side_f, side_p, out):
    cells = own_f.shape[0] // CELL
    for slot in range(wanted.shape[0] // 2):
        block, cell = wanted[slot] // cells, wanted[slot] % cells

        def put(feats, places, slot=slot, cell=cell):
            base = slot * PACKED
            out[base : base + CELL, :] = cell_at(feats, cell)
            rows = jnp.concatenate([tall(place_at(places, cell)), jnp.zeros((8, CELL), F32)], axis=0)
            out[base + CELL : base + PACKED, :] = rows.astype(BF)

        pl.when(block == 2)(functools.partial(put, own_f, own_p))
        pl.when(block == 3)(functools.partial(put, side_f, side_p))


def tile_kernel(
    stage, first, second, live_a, live_b, own_f, own_p, *refs
):
    if stage == 0:
        remote = ()
    elif stage == 1:
        remote, refs = refs[:3], refs[3:]
    else:
        remote, refs = refs[:2], refs[2:]
    (w_a, w_b, radial, mix, out_w, total, grads,
     flip, mix_t, mix_o, scale_o, last, onehot, proj_r, proj_l, dist, slope_sum, read_sum, fb, pa, pb, tiles, steps) = refs
    cells = own_f.shape[0] // CELL
    count = first.shape[0]
    width = ROWS * CELL

    flip[0] = jnp.transpose(w_a[...].astype(F32)).astype(BF)
    flip[1] = jnp.transpose(w_b[...].astype(F32)).astype(BF)
    mix_f = mix[...].astype(F32)
    mix_t[...] = (jnp.transpose(mix_f) * 0.5).astype(BF)
    mix_o[...] = (mix_f * 0.25).astype(BF)
    scale_o[...] = jnp.transpose(jnp.broadcast_to(out_w[...] / CELL, (CELL, CELL)))
    high = out_w[...].astype(BF)
    low = (out_w[...] - high.astype(F32)).astype(BF)
    pad = jnp.zeros((6, CELL), F32)
    left = jnp.concatenate([radial[...].astype(F32), jnp.zeros((8, CELL), F32)], axis=0)
    right = jnp.concatenate([jnp.zeros((NB, CELL), F32), high.astype(F32), low.astype(F32), pad], axis=0)
    last[...] = jnp.concatenate([left, right], axis=1).astype(BF)
    radial_h = radial[...].astype(F32) * 0.5
    row_of = lax.broadcasted_iota(jnp.int32, (NB, width), 0)
    lane_of = lax.broadcasted_iota(jnp.int32, (NB, width), 1) // CELL
    onehot[...] = jnp.where(row_of == lane_of, 1.0, 0.0).astype(BF)
    centers = lax.broadcasted_iota(jnp.int32, (NB, CELL), 0).astype(F32) * (6.75 / NB)

    if stage == 0:
        total[...] = jnp.zeros_like(total)
    else:
        total[...] = remote[-1][...]

    picked, own_seen = jnp.int32(0), jnp.int32(0)
    for t in range(count):
        block = second[t] // cells
        own = block == 0
        if stage == 0:
            take = own & (own_seen < EARLY)
        elif stage == 1:
            take = (own & (own_seen >= EARLY)) | (block == 1)
        else:
            take = block >= 2
        own_seen = own_seen + own.astype(jnp.int32)
        tiles[picked] = jnp.int32(t)
        picked = picked + take.astype(jnp.int32)

    def prepare(s, so_far):
        t = tiles[s]
        cell = second[t] % cells
        pa[s] = tall(place_at(own_p, first[t]))
        if stage == 2:
            base = pl.multiple_of(t * PACKED, 16)
            fb[...] = remote[0][pl.ds(base, CELL), :]
            rest = remote[0][pl.ds(pl.multiple_of(base + CELL, 16), 16), :]
            pb[s] = rest.astype(F32)[0:8]
        else:
            def bring(feats, places):
                fb[...] = cell_at(feats, cell)
                pb[s] = tall(place_at(places, cell))

            if stage == 0:
                bring(own_f, own_p)
            else:
                pl.when(second[t] < cells)(functools.partial(bring, own_f, own_p))
                pl.when(second[t] >= cells)(functools.partial(bring, remote[0], remote[1]))
        num_a, num_b = live_a[t], live_b[t]
        swap = num_a > num_b
        feats_a, feats_b = cell_at(own_f, first[t]), fb[...]
        rows_f = jnp.where(swap, feats_b, feats_a)
        lanes_f = jnp.where(swap, feats_a, feats_b)
        rows_p, lanes_p = jnp.where(swap, pb[s], pa[s]), jnp.where(swap, pa[s], pb[s])
        w_r = jnp.where(swap, w_b[...], w_a[...])
        w_l = jnp.where(swap, flip[0], flip[1])
        proj_r[s] = dot(rows_f, w_r).astype(BF).astype(F32) * 0.5
        proj_l[s] = lax.dot_general(w_l, lanes_f, LAST, preferred_element_type=F32).astype(BF).astype(F32) * 0.5
        tall_p = jnp.transpose(rows_p)
        gaps = [tall_p[:, c : c + 1] - lanes_p[c : c + 1, :] for c in range(3)]
        dist[s] = gaps[0] * gaps[0] + gaps[1] * gaps[1] + gaps[2] * gaps[2]
        n = (jnp.minimum(num_a, num_b) + ROWS - 1) // ROWS
        steps[s] = n
        return so_far + n

    trips = lax.fori_loop(0, picked, prepare, jnp.int32(0))

    def edges(_, where):
        s, g = where
        at = pl.multiple_of(g * ROWS, ROWS)
        r2 = dist[s, pl.ds(at, ROWS), :]
        weights = jnp.transpose(
            jnp.concatenate([radial_h, proj_r[s, pl.ds(at, ROWS), :]], axis=0)
        ).astype(BF)
        offset = jnp.concatenate(
            [jnp.broadcast_to(r2[k : k + 1, :], (NB, CELL)) - centers for k in range(ROWS)], axis=1
        )
        basis = jnp.exp(-2.0 * offset * offset)
        inputs = jnp.concatenate([basis.astype(BF), onehot[...]], axis=0)
        half = dot(weights, inputs) + jnp.concatenate([proj_l[s]] * ROWS, axis=1)
        bend = jnp.tanh(half)
        up = 1 + bend
        latent = half * up
        slope = up + latent * (1 - bend)
        pre = dot(mix_t[...], latent.astype(BF))
        bend = jnp.tanh(pre)
        up = 1 + bend
        act = pre * up
        near = 1.0 - r2 / 8.0
        near = near * near
        envelope = jnp.concatenate([near[k : k + 1, :] for k in range(ROWS)], axis=1)
        d_pre = envelope * jnp.concatenate([scale_o[...]] * ROWS, axis=1) * (up + act * (1 - bend))
        d_latent = dot(mix_o[...], d_pre.astype(BF))
        d_summed = (d_latent * slope).astype(BF)
        act = act.astype(BF)
        both = dot(last[...], jnp.concatenate([d_summed, act], axis=0))
        d_r2 = jnp.sum(both[:NB] * (basis * offset), axis=0, keepdims=True)
        readout = both[NB : NB + 1] + both[NB + 1 : NB + 2]
        cut = [slice(k * CELL, (k + 1) * CELL) for k in range(ROWS)]
        slope_sum[s, pl.ds(at, ROWS), :] = jnp.concatenate([d_r2[:, c] for c in cut], axis=0)
        read_sum[s, pl.ds(at, ROWS), :] = jnp.concatenate([readout[:, c] for c in cut], axis=0)
        over = g + 1 >= steps[s]
        return jnp.where(over, jnp.minimum(s + 1, count - 1), s), jnp.where(over, 0, g + 1)

    lax.fori_loop(0, trips, edges, (jnp.int32(0), jnp.int32(0)))

    row_at = lax.broadcasted_iota(jnp.int32, (CELL, CELL), 0)
    lane_at = lax.broadcasted_iota(jnp.int32, (CELL, CELL), 1)

    def finish(s, _):
        t = tiles[s]
        num_a, num_b = live_a[t], live_b[t]
        swap = num_a > num_b
        rows_p, lanes_p = jnp.where(swap, pb[s], pa[s]), jnp.where(swap, pa[s], pb[s])
        live = (row_at < jnp.minimum(num_a, num_b)) & (lane_at < jnp.maximum(num_a, num_b))
        near = 1.0 - dist[s] / 8.0
        pull = 2.0 * (-4.0 * slope_sum[s] - near * (0.25 / CELL) * read_sum[s])
        pull = jnp.where(live, pull, 0.0)
        high = pull.astype(BF)
        low = (pull - high.astype(F32)).astype(BF)

        def with_ones(places):
            rows = jnp.concatenate([places[0:3], jnp.ones((1, CELL), F32), jnp.zeros((4, CELL), F32)], axis=0)
            rows = rows.astype(BF)
            return jnp.concatenate([rows, rows], axis=1)

        over_lanes = lax.dot_general(
            with_ones(lanes_p), jnp.concatenate([high, low], axis=1), LAST, preferred_element_type=F32
        )
        over_rows = dot(with_ones(rows_p), jnp.concatenate([high, low], axis=0))
        grad_r = rows_p * over_lanes[3:4] - over_lanes
        grad_l = lanes_p * over_rows[3:4] - over_rows
        grad_a = jnp.where(swap, grad_l, grad_r)
        grad_b = jnp.where(swap, grad_r, grad_l)
        here = pl.ds(pl.multiple_of(first[t] * CELL, CELL), CELL)
        total[:, here] = total[:, here] + grad_a[0:3]
        if stage != 2:
            @pl.when(second[t] < cells)
            def _():
                there = pl.ds(pl.multiple_of(second[t] * CELL, CELL), CELL)
                total[:, there] = total[:, there] + grad_b[0:3]
        grads[t] = grad_b
        return 0

    lax.fori_loop(0, picked, finish, 0)


def final_kernel(asked, asked_up, total, side, upper, corner, out):
    cells = total.shape[1] // CELL
    count = asked.shape[0]
    out[...] = -total[...]

    def take(wanted, block, got, slot):
        @pl.when(wanted // cells == block)
        def _():
            here = pl.ds(pl.multiple_of(wanted % cells * CELL, CELL), CELL)
            out[:, here] = out[:, here] - got[slot][0:3]

    for slot in range(count):
        take(asked[slot], 1, side, slot)
        take(asked_up[slot], 2, upper, slot)
        take(asked_up[count + slot], 3, corner, slot)


def called(kernel, prefetch, operands, out_shape, scratch=(), work=1.0, name=None):
    return pl.pallas_call(
        kernel,
        grid_spec=pltpu.PrefetchScalarGridSpec(
            num_scalar_prefetch=len(prefetch),
            grid=(1,),
            in_specs=[VMEM] * len(operands),
            out_specs=jax.tree.map(lambda _: VMEM, out_shape),
            scratch_shapes=list(scratch),
        ),
        out_shape=out_shape,
        compiler_params=pltpu.CompilerParams(vmem_limit_bytes=40 << 20),
        cost_estimate=pl.CostEstimate(flops=int(work * 1e9), bytes_accessed=1 << 20, transcendentals=0),
        name=name,
    )(*prefetch, *operands)


def on_device(
    positions,
    features,
    tile_first,
    tile_second,
    count_first,
    count_second,
    w_first,
    w_second,
    radial_weight,
    mix_weight,
    out_weight,
):
    slots = positions.shape[1]
    count = tile_first.shape[0]
    asked = shifted(tile_second, 0, -1)
    side_f = shifted(features, 0, 1)
    side_p = shifted(positions, 0, 1)
    asked_up = shifted(jnp.concatenate([tile_second, asked]), -1, 0)

    scalars = (tile_first, tile_second, count_first, count_second)
    weights = (w_first, w_second, radial_weight, mix_weight, out_weight.reshape(1, -1))
    out_shape = (
        jax.ShapeDtypeStruct((3, slots), F32),
        jax.ShapeDtypeStruct((count, 8, CELL), F32),
    )
    square = (count, CELL, CELL)
    scratch = [
        pltpu.VMEM((2, CELL, CELL), BF),
        pltpu.VMEM((CELL, CELL), BF),
        pltpu.VMEM((CELL, CELL), BF),
        pltpu.VMEM((CELL, CELL), F32),
        pltpu.VMEM((24, 2 * CELL), BF),
        pltpu.VMEM((NB, ROWS * CELL), BF),
        *[pltpu.VMEM(square, F32)] * 5,
        pltpu.VMEM((CELL, CELL), BF),
        *[pltpu.VMEM((count, 8, CELL), F32)] * 2,
        pltpu.SMEM((count + 1,), jnp.int32),
        pltpu.SMEM((count,), jnp.int32),
    ]

    def tiles(stage, extra, work):
        operands = (features, positions, *extra, *weights)
        return called(
            functools.partial(tile_kernel, stage), scalars, operands, out_shape, scratch, work, f"tiles{stage}"
        )

    total, _ = tiles(0, (), 6.0)
    packed = called(
        pack_kernel,
        (asked_up,),
        (features, positions, side_f, side_p),
        jax.ShapeDtypeStruct((count * PACKED, CELL), BF),
        name="pack",
    )
    upper_cells = shifted(packed, 1, 0)
    total, grads = tiles(1, (side_f, side_p, total), 8.0)
    from_side = shifted(grads, 0, -1)
    total, grads = tiles(2, (upper_cells, total), 16.0)
    from_upper = shifted(grads, -1, 0)
    from_corner = shifted(grads, -1, -1)
    return called(
        final_kernel,
        (asked, asked_up),
        (total, from_side, from_upper, from_corner),
        jax.ShapeDtypeStruct((3, slots), F32),
        name="final",
    )


def solution(mesh):
    whole = ("grp", "dev")
    in_specs = (P(None, whole), P(whole, None), *[P(whole)] * 4, *[P()] * 5)
    return jax.shard_map(
        on_device, mesh=mesh, in_specs=in_specs, out_specs=P(None, whole), check_vma=False
    )
```

```python
import functools

import jax
import jax.numpy as jnp
from jax import lax
from jax.experimental import pallas as pl
from jax.experimental.pallas import tpu as pltpu
from jax.sharding import PartitionSpec as P

CELL = 128
NB = 16
ROWS = 16
PACKED = CELL + 16
EARLY = 8
F32, BF = jnp.float32, jnp.bfloat16
LAST = (((1,), (1,)), ((), ()))
VMEM = pl.BlockSpec(memory_space=pltpu.VMEM)


def shifted(array, groups, members):
    n_grp, n_dev = lax.axis_size("grp"), lax.axis_size("dev")
    if groups == 0:
        return lax.ppermute(array, "dev", [(i, (i + members) % n_dev) for i in range(n_dev)])
    if members == 0:
        return lax.ppermute(array, "grp", [(i, (i + groups) % n_grp) for i in range(n_grp)])
    pairs = [
        (g * n_dev + d, (g + groups) % n_grp * n_dev + (d + members) % n_dev)
        for g in range(n_grp)
        for d in range(n_dev)
    ]
    return lax.ppermute(array, ("grp", "dev"), pairs)


def dot(a, b):
    return jnp.dot(a, b, preferred_element_type=F32)


def cell_at(ref, cell):
    return ref[pl.ds(pl.multiple_of(cell * CELL, CELL), CELL), :]


def place_at(ref, cell):
    return ref[:, pl.ds(pl.multiple_of(cell * CELL, CELL), CELL)]


def tall(places):
    return jnp.concatenate([places.astype(F32), jnp.zeros((5, CELL), F32)], axis=0)


def pack_kernel(wanted, own_f, own_p, side_f, side_p, out):
    cells = own_f.shape[0] // CELL
    for slot in range(wanted.shape[0]):
        block, cell = wanted[slot] // cells, wanted[slot] % cells

        def put(feats, places, slot=slot, cell=cell):
            base = slot * PACKED
            out[base : base + CELL, :] = cell_at(feats, cell)
            rows = jnp.concatenate([tall(place_at(places, cell)), jnp.zeros((8, CELL), F32)], axis=0)
            out[base + CELL : base + PACKED, :] = rows.astype(BF)

        pl.when(block == 2)(functools.partial(put, own_f, own_p))
        pl.when(block == 3)(functools.partial(put, side_f, side_p))


def tile_kernel(
    stage, first, second, live_a, live_b, own_f, own_p, *refs
):
    extra = (0, 3, 2)[stage]
    remote, refs = refs[:extra], refs[extra:]
    outs = (1, 2, 2)[stage]
    (w_a, w_b, radial, mix, out_w), refs = refs[:5], refs[5:]
    total, side = refs[0], refs[outs - 1]
    refs = refs[outs:]
    if stage == 0:
        given = (own_f, own_p, w_a, w_b, radial, mix, out_w)
        own_f, own_p, w_a, w_b, radial, mix, out_w = held = refs[-8:-1]
        copies = [pltpu.make_async_copy(*pair, refs[-1].at[k]) for k, pair in enumerate(zip(given, held))]
        for copy in copies:
            copy.start()
        for copy in copies:
            copy.wait()
        refs = refs[:-8]
    (
     flip, mix_t, mix_o, scale_o, last, onehot, proj_r, proj_l, dist, slope_sum, read_sum, fb, pa, pb, tiles, steps) = refs
    cells = own_f.shape[0] // CELL
    count = first.shape[0]
    width = ROWS * CELL

    flip[0] = jnp.transpose(w_a[...].astype(F32)).astype(BF)
    flip[1] = jnp.transpose(w_b[...].astype(F32)).astype(BF)
    mix_f = mix[...].astype(F32)
    mix_t[...] = (jnp.transpose(mix_f) * 0.5).astype(BF)
    mix_o[...] = (mix_f * 0.25).astype(BF)
    scale_o[...] = jnp.transpose(jnp.broadcast_to(out_w[...] / CELL, (CELL, CELL)))
    high = out_w[...].astype(BF)
    low = (out_w[...] - high.astype(F32)).astype(BF)
    pad = jnp.zeros((6, CELL), F32)
    left = jnp.concatenate([radial[...].astype(F32), jnp.zeros((8, CELL), F32)], axis=0)
    right = jnp.concatenate([jnp.zeros((NB, CELL), F32), high.astype(F32), low.astype(F32), pad], axis=0)
    last[...] = jnp.concatenate([left, right], axis=1).astype(BF)
    radial_h = radial[...].astype(F32) * 0.5
    row_of = lax.broadcasted_iota(jnp.int32, (NB, width), 0)
    lane_of = lax.broadcasted_iota(jnp.int32, (NB, width), 1) // CELL
    onehot[...] = jnp.where(row_of == lane_of, 1.0, 0.0).astype(BF)
    centers = lax.broadcasted_iota(jnp.int32, (NB, CELL), 0).astype(F32) * (6.75 / NB)

    if stage == 0:
        total[...] = jnp.zeros_like(total)
    else:
        total[...] = remote[-1][...]
    if stage == 1:
        side[...] = jnp.zeros_like(side)

    picked, early = jnp.int32(0), jnp.int32(0)
    for t in range(count):
        block = second[t] // cells
        need = (jnp.minimum(live_a[t], live_b[t]) + ROWS - 1) // ROWS
        soon = (block == 0) & (early + need <= EARLY)
        early = early + jnp.where(soon, need, 0)
        take = (soon, (block < 2) & ~soon, block >= 2)[stage]
        tiles[picked] = jnp.int32(t)
        picked = picked + take.astype(jnp.int32)

    def prepare(s, so_far):
        t = tiles[s]
        cell = second[t] % cells
        pa[s] = tall(place_at(own_p, first[t]))
        if stage == 2:
            base = pl.multiple_of(t * PACKED, 16)
            fb[...] = remote[0][pl.ds(base, CELL), :]
            rest = remote[0][pl.ds(pl.multiple_of(base + CELL, 16), 16), :]
            pb[s] = rest.astype(F32)[0:8]
        else:
            def bring(feats, places):
                fb[...] = cell_at(feats, cell)
                pb[s] = tall(place_at(places, cell))

            if stage == 0:
                bring(own_f, own_p)
            else:
                pl.when(second[t] < cells)(functools.partial(bring, own_f, own_p))
                pl.when(second[t] >= cells)(functools.partial(bring, remote[0], remote[1]))
        num_a, num_b = live_a[t], live_b[t]
        swap = num_a > num_b
        feats_a, feats_b = cell_at(own_f, first[t]), fb[...]
        rows_f = jnp.where(swap, feats_b, feats_a)
        lanes_f = jnp.where(swap, feats_a, feats_b)
        rows_p, lanes_p = jnp.where(swap, pb[s], pa[s]), jnp.where(swap, pa[s], pb[s])
        w_r = jnp.where(swap, w_b[...], w_a[...])
        w_l = jnp.where(swap, flip[0], flip[1])
        proj_r[s] = dot(rows_f, w_r).astype(BF).astype(F32) * 0.5
        proj_l[s] = lax.dot_general(w_l, lanes_f, LAST, preferred_element_type=F32).astype(BF).astype(F32) * 0.5
        tall_p = jnp.transpose(rows_p)
        gaps = [tall_p[:, c : c + 1] - lanes_p[c : c + 1, :] for c in range(3)]
        dist[s] = gaps[0] * gaps[0] + gaps[1] * gaps[1] + gaps[2] * gaps[2]
        n = (jnp.minimum(num_a, num_b) + ROWS - 1) // ROWS
        steps[s] = n
        return so_far + n

    trips = lax.fori_loop(0, picked, prepare, jnp.int32(0))

    def edges(_, where):
        s, g = where
        at = pl.multiple_of(g * ROWS, ROWS)
        r2 = dist[s, pl.ds(at, ROWS), :]
        weights = jnp.transpose(
            jnp.concatenate([radial_h, proj_r[s, pl.ds(at, ROWS), :]], axis=0)
        ).astype(BF)
        offset = jnp.concatenate(
            [jnp.broadcast_to(r2[k : k + 1, :], (NB, CELL)) - centers for k in range(ROWS)], axis=1
        )
        basis = jnp.exp(-2.0 * offset * offset)
        inputs = jnp.concatenate([basis.astype(BF), onehot[...]], axis=0)
        half = dot(weights, inputs) + jnp.concatenate([proj_l[s]] * ROWS, axis=1)
        bend = jnp.tanh(half)
        up = 1 + bend
        latent = half * up
        slope = up + latent * (1 - bend)
        pre = dot(mix_t[...], latent.astype(BF))
        bend = jnp.tanh(pre)
        up = 1 + bend
        act = pre * up
        near = 1.0 - r2 / 8.0
        near = near * near
        envelope = jnp.concatenate([near[k : k + 1, :] for k in range(ROWS)], axis=1)
        d_pre = envelope * jnp.concatenate([scale_o[...]] * ROWS, axis=1) * (up + act * (1 - bend))
        d_latent = dot(mix_o[...], d_pre.astype(BF))
        d_summed = (d_latent * slope).astype(BF)
        act = act.astype(BF)
        both = dot(last[...], jnp.concatenate([d_summed, act], axis=0))
        d_r2 = jnp.sum(both[:NB] * (basis * offset), axis=0, keepdims=True)
        readout = both[NB : NB + 1] + both[NB + 1 : NB + 2]
        cut = [slice(k * CELL, (k + 1) * CELL) for k in range(ROWS)]
        slope_sum[s, pl.ds(at, ROWS), :] = jnp.concatenate([d_r2[:, c] for c in cut], axis=0)
        read_sum[s, pl.ds(at, ROWS), :] = jnp.concatenate([readout[:, c] for c in cut], axis=0)
        over = g + 1 >= steps[s]
        return jnp.where(over, jnp.minimum(s + 1, count - 1), s), jnp.where(over, 0, g + 1)

    lax.fori_loop(0, trips, edges, (jnp.int32(0), jnp.int32(0)))

    row_at = lax.broadcasted_iota(jnp.int32, (CELL, CELL), 0)
    lane_at = lax.broadcasted_iota(jnp.int32, (CELL, CELL), 1)

    def finish(s, _):
        t = tiles[s]
        num_a, num_b = live_a[t], live_b[t]
        swap = num_a > num_b
        rows_p, lanes_p = jnp.where(swap, pb[s], pa[s]), jnp.where(swap, pa[s], pb[s])
        live = (row_at < jnp.minimum(num_a, num_b)) & (lane_at < jnp.maximum(num_a, num_b))
        near = 1.0 - dist[s] / 8.0
        pull = 2.0 * (-4.0 * slope_sum[s] - near * (0.25 / CELL) * read_sum[s])
        pull = jnp.where(live, pull, 0.0)
        high = pull.astype(BF)
        low = (pull - high.astype(F32)).astype(BF)

        def with_ones(places):
            rows = jnp.concatenate([places[0:3], jnp.ones((1, CELL), F32), jnp.zeros((4, CELL), F32)], axis=0)
            rows = rows.astype(BF)
            return jnp.concatenate([rows, rows], axis=1)

        over_lanes = lax.dot_general(
            with_ones(lanes_p), jnp.concatenate([high, low], axis=1), LAST, preferred_element_type=F32
        )
        over_rows = dot(with_ones(rows_p), jnp.concatenate([high, low], axis=0))
        grad_r = rows_p * over_lanes[3:4] - over_lanes
        grad_l = lanes_p * over_rows[3:4] - over_rows
        grad_a = jnp.where(swap, grad_l, grad_r)
        grad_b = jnp.where(swap, grad_r, grad_l)
        here = pl.ds(pl.multiple_of(first[t] * CELL, CELL), CELL)
        total[:, here] = total[:, here] + grad_a[0:3]
        there = pl.ds(pl.multiple_of(second[t] % cells * CELL, CELL), CELL)

        def add(sums):
            sums[:, there] = sums[:, there] + grad_b[0:3]

        if stage == 0:
            add(total)
        elif stage == 1:
            pl.when(second[t] < cells)(functools.partial(add, total))
            pl.when(second[t] >= cells)(functools.partial(add, side))
        else:
            side[t] = grad_b
        return 0

    lax.fori_loop(0, picked, finish, 0)


def hand_kernel(wanted, total, side, got, total_out, side_out):
    cells = total.shape[1] // CELL
    total_out[...] = total[...]
    side_out[...] = side[...]
    for slot in range(wanted.shape[0]):
        block = wanted[slot] // cells
        here = pl.ds(pl.multiple_of(wanted[slot] % cells * CELL, CELL), CELL)

        def add(sums, slot=slot, here=here):
            sums[:, here] = sums[:, here] + got[slot][0:3]

        pl.when(block == 2)(functools.partial(add, total_out))
        pl.when(block == 3)(functools.partial(add, side_out))


def last_kernel(total, got, out):
    out[...] = -(total[...] + got[...])


def called(kernel, prefetch, operands, out_shape, scratch=(), work=1.0, name=None, bring=False):
    if bring:
        scratch = [*scratch, *[pltpu.VMEM(x.shape, x.dtype) for x in operands]]
        scratch.append(pltpu.SemaphoreType.DMA((len(operands),)))
    return pl.pallas_call(
        kernel,
        grid_spec=pltpu.PrefetchScalarGridSpec(
            num_scalar_prefetch=len(prefetch),
            grid=(1,),
            in_specs=[pl.BlockSpec(memory_space=pltpu.HBM) if bring else VMEM] * len(operands),
            out_specs=jax.tree.map(lambda _: VMEM, out_shape),
            scratch_shapes=list(scratch),
        ),
        out_shape=out_shape,
        compiler_params=pltpu.CompilerParams(vmem_limit_bytes=40 << 20),
        cost_estimate=pl.CostEstimate(flops=int(work * 1e9), bytes_accessed=1 << 20, transcendentals=0),
        name=name,
    )(*prefetch, *operands)


def on_device(
    positions,
    features,
    tile_first,
    tile_second,
    count_first,
    count_second,
    w_first,
    w_second,
    radial_weight,
    mix_weight,
    out_weight,
):
    slots = positions.shape[1]
    count = tile_first.shape[0]
    side_f = shifted(features, 0, 1)
    side_p = shifted(positions, 0, 1)
    asked = shifted(tile_second, -1, 0)

    scalars = (tile_first, tile_second, count_first, count_second)
    weights = (w_first, w_second, radial_weight, mix_weight, out_weight.reshape(1, -1))
    sums = jax.ShapeDtypeStruct((3, slots), F32)
    square = (count, CELL, CELL)
    scratch = [
        pltpu.VMEM((2, CELL, CELL), BF),
        pltpu.VMEM((CELL, CELL), BF),
        pltpu.VMEM((CELL, CELL), BF),
        pltpu.VMEM((CELL, CELL), F32),
        pltpu.VMEM((24, 2 * CELL), BF),
        pltpu.VMEM((NB, ROWS * CELL), BF),
        *[pltpu.VMEM(square, F32)] * 5,
        pltpu.VMEM((CELL, CELL), BF),
        *[pltpu.VMEM((count, 8, CELL), F32)] * 2,
        pltpu.SMEM((count + 1,), jnp.int32),
        pltpu.SMEM((count,), jnp.int32),
    ]

    def tiles(stage, extra, outs, work):
        operands = (features, positions, *extra, *weights)
        return called(
            functools.partial(tile_kernel, stage), scalars, operands, outs, scratch, work,
            f"tiles{stage}", bring=stage == 0,
        )

    (total,) = tiles(0, (), (sums,), 8.0)
    packed = called(
        pack_kernel,
        (asked,),
        (features, positions, side_f, side_p),
        jax.ShapeDtypeStruct((count * PACKED, CELL), BF),
        name="pack",
    )
    upper_cells = shifted(packed, 1, 0)
    total, side = tiles(1, (side_f, side_p, total), (sums, sums), 8.0)
    grads = jax.ShapeDtypeStruct((count, 8, CELL), F32)
    total, grads = tiles(2, (upper_cells, total), (sums, grads), 16.0)
    from_upper = shifted(grads, -1, 0)
    total, side = called(hand_kernel, (asked,), (total, side, from_upper), (sums, sums), name="hand")
    from_side = shifted(side, 0, -1)
    return called(last_kernel, (), (total, from_side), sums, name="last")


def solution(mesh):
    whole = ("grp", "dev")
    in_specs = (P(None, whole), P(whole, None), *[P(whole)] * 4, *[P()] * 5)
    return jax.shard_map(
        on_device, mesh=mesh, in_specs=in_specs, out_specs=P(None, whole), check_vma=False
    )
```

```python
import functools

import jax
import jax.numpy as jnp
from jax import lax
from jax.experimental import pallas as pl
from jax.experimental.pallas import tpu as pltpu
from jax.sharding import PartitionSpec as P

CELL = 128
NB = 16
UNIT = 8
UNITS = 2
ROWS = UNIT * UNITS
PACKED = CELL + 16
EARLY = 16
F32, BF = jnp.float32, jnp.bfloat16
LAST = (((1,), (1,)), ((), ()))
VMEM = pl.BlockSpec(memory_space=pltpu.VMEM)


def shifted(array, groups, members):
    n_grp, n_dev = lax.axis_size("grp"), lax.axis_size("dev")
    if groups == 0:
        return lax.ppermute(array, "dev", [(i, (i + members) % n_dev) for i in range(n_dev)])
    if members == 0:
        return lax.ppermute(array, "grp", [(i, (i + groups) % n_grp) for i in range(n_grp)])
    pairs = [
        (g * n_dev + d, (g + groups) % n_grp * n_dev + (d + members) % n_dev)
        for g in range(n_grp)
        for d in range(n_dev)
    ]
    return lax.ppermute(array, ("grp", "dev"), pairs)


def dot(a, b):
    return jnp.dot(a, b, preferred_element_type=F32)


def cell_at(ref, cell):
    return ref[pl.ds(pl.multiple_of(cell * CELL, CELL), CELL), :]


def place_at(ref, cell):
    return ref[:, pl.ds(pl.multiple_of(cell * CELL, CELL), CELL)]


def tall(places):
    return jnp.concatenate([places.astype(F32), jnp.zeros((5, CELL), F32)], axis=0)


def pack_kernel(wanted, own_f, own_p, side_f, side_p, out):
    cells = own_f.shape[0] // CELL
    for slot in range(wanted.shape[0]):
        block, cell = wanted[slot] // cells, wanted[slot] % cells

        def put(feats, places, slot=slot, cell=cell):
            base = slot * PACKED
            out[base : base + CELL, :] = cell_at(feats, cell)
            rows = jnp.concatenate([tall(place_at(places, cell)), jnp.zeros((8, CELL), F32)], axis=0)
            out[base + CELL : base + PACKED, :] = rows.astype(BF)

        pl.when(block == 2)(functools.partial(put, own_f, own_p))
        pl.when(block == 3)(functools.partial(put, side_f, side_p))


def tile_kernel(
    stage, first, second, live_a, live_b, own_f, own_p, *refs
):
    extra = (0, 3, 2)[stage]
    remote, refs = refs[:extra], refs[extra:]
    outs = (1, 2, 2)[stage]
    (w_a, w_b, radial, mix, out_w), refs = refs[:5], refs[5:]
    total, side = refs[0], refs[outs - 1]
    refs = refs[outs:]
    if stage == 0:
        given = (own_f, own_p, w_a, w_b, radial, mix, out_w)
        own_f, own_p, w_a, w_b, radial, mix, out_w = held = refs[-8:-1]
        copies = [pltpu.make_async_copy(*pair, refs[-1].at[k]) for k, pair in enumerate(zip(given, held))]
        for copy in copies:
            copy.start()
        for copy in copies:
            copy.wait()
        refs = refs[:-8]
    (
     flip, mix_t, mix_o, scale_o, last, onehot, proj_r, proj_l, dist, slope_sum, read_sum, fb, pa, pb, near_rows, half_s, tilt_s, tiles, steps) = refs
    cells = own_f.shape[0] // CELL
    count = first.shape[0]
    width = ROWS * CELL

    flip[0] = jnp.transpose(w_a[...].astype(F32)).astype(BF)
    flip[1] = jnp.transpose(w_b[...].astype(F32)).astype(BF)
    mix_f = mix[...].astype(F32)
    mix_t[...] = (jnp.transpose(mix_f) * 0.5).astype(BF)
    mix_o[...] = (mix_f * 0.25).astype(BF)
    scale_o[...] = jnp.transpose(jnp.broadcast_to(out_w[...] / CELL, (CELL, CELL)))
    high = out_w[...].astype(BF)
    low = (out_w[...] - high.astype(F32)).astype(BF)
    pad = jnp.zeros((6, CELL), F32)
    left = jnp.concatenate([radial[...].astype(F32), jnp.zeros((8, CELL), F32)], axis=0)
    right = jnp.concatenate([jnp.zeros((NB, CELL), F32), high.astype(F32), low.astype(F32), pad], axis=0)
    last[...] = jnp.concatenate([left, right], axis=1).astype(BF)
    radial_h = radial[...].astype(F32) * 0.5
    row_of = lax.broadcasted_iota(jnp.int32, (ROWS, width), 0)
    lane_of = lax.broadcasted_iota(jnp.int32, (ROWS, width), 1) // CELL
    onehot[...] = jnp.where(row_of == lane_of, 1.0, 0.0).astype(BF)
    centers = lax.broadcasted_iota(jnp.int32, (NB, CELL), 0).astype(F32) * (6.75 / NB)

    if stage == 0:
        total[...] = jnp.zeros_like(total)
    else:
        total[...] = remote[-1][...]
    if stage == 1:
        side[...] = jnp.zeros_like(side)

    picked, early = jnp.int32(0), jnp.int32(0)
    for t in range(count):
        block = second[t] // cells
        need = (jnp.minimum(live_a[t], live_b[t]) + UNIT - 1) // UNIT
        soon = (block == 0) & (early + need <= EARLY)
        early = early + jnp.where(soon, need, 0)
        take = (soon, (block < 2) & ~soon, block >= 2)[stage]
        tiles[picked] = jnp.int32(t)
        picked = picked + take.astype(jnp.int32)

    def prepare(s, so_far):
        t = tiles[s]
        cell = second[t] % cells
        pa[s] = tall(place_at(own_p, first[t]))
        if stage == 2:
            base = pl.multiple_of(t * PACKED, 16)
            fb[...] = remote[0][pl.ds(base, CELL), :]
            rest = remote[0][pl.ds(pl.multiple_of(base + CELL, 16), 16), :]
            pb[s] = rest.astype(F32)[0:8]
        else:
            def bring(feats, places):
                fb[...] = cell_at(feats, cell)
                pb[s] = tall(place_at(places, cell))

            if stage == 0:
                bring(own_f, own_p)
            else:
                pl.when(second[t] < cells)(functools.partial(bring, own_f, own_p))
                pl.when(second[t] >= cells)(functools.partial(bring, remote[0], remote[1]))
        num_a, num_b = live_a[t], live_b[t]
        swap = num_a > num_b
        feats_a, feats_b = cell_at(own_f, first[t]), fb[...]
        rows_f = jnp.where(swap, feats_b, feats_a)
        lanes_f = jnp.where(swap, feats_a, feats_b)
        rows_p, lanes_p = jnp.where(swap, pb[s], pa[s]), jnp.where(swap, pa[s], pb[s])
        w_r = jnp.where(swap, w_b[...], w_a[...])
        w_l = jnp.where(swap, flip[0], flip[1])
        proj_r[s] = dot(rows_f, w_r).astype(BF).astype(F32) * 0.5
        proj_l[s] = lax.dot_general(w_l, lanes_f, LAST, preferred_element_type=F32).astype(BF).astype(F32) * 0.5
        tall_p = jnp.transpose(rows_p)
        gaps = [tall_p[:, c : c + 1] - lanes_p[c : c + 1, :] for c in range(3)]
        dist[s] = gaps[0] * gaps[0] + gaps[1] * gaps[1] + gaps[2] * gaps[2]
        n = (jnp.minimum(num_a, num_b) + UNIT - 1) // UNIT
        steps[s] = n
        return so_far + n

    units = lax.fori_loop(0, picked, prepare, jnp.int32(0))

    proj_r[picked, 0:UNIT, :] = jnp.zeros((UNIT, CELL), F32)
    dist[picked, 0:UNIT, :] = jnp.zeros((UNIT, CELL), F32)

    def after(s, g):
        over = g + 1 >= steps[s]
        return jnp.where(over, s + 1, s), jnp.where(over, 0, g + 1)

    def rows_of(ref, where):
        return [ref[s, pl.ds(pl.multiple_of(g * UNIT, UNIT), UNIT), :] for s, g in where]

    def enter(where):
        r2 = jnp.concatenate(rows_of(dist, where), axis=0)
        weights = jnp.transpose(jnp.concatenate([radial_h, *rows_of(proj_r, where)], axis=0)).astype(BF)
        offset = jnp.concatenate(
            [jnp.broadcast_to(r2[k : k + 1, :], (NB, CELL)) - centers for k in range(ROWS)], axis=1
        )
        basis = jnp.exp(-2.0 * offset * offset)
        inputs = jnp.concatenate([basis.astype(BF), onehot[...]], axis=0)
        lanes = jnp.concatenate([proj_l[s] for s, g in where for _ in range(UNIT)], axis=1)
        return r2, dot(weights, inputs) + lanes, basis * offset

    def rest(where, r2, half, tilt):
        bend = jnp.tanh(half)
        up = 1 + bend
        latent = half * up
        slope = up + latent * (1 - bend)
        pre = dot(mix_t[...], latent.astype(BF))
        bend = jnp.tanh(pre)
        up = 1 + bend
        act = pre * up
        near = 1.0 - r2 / 8.0
        near = near * near
        envelope = jnp.concatenate([near[k : k + 1, :] for k in range(ROWS)], axis=1)
        d_pre = envelope * jnp.concatenate([scale_o[...]] * ROWS, axis=1) * (up + act * (1 - bend))
        d_latent = dot(mix_o[...], d_pre.astype(BF))
        d_summed = (d_latent * slope).astype(BF)
        both = dot(last[...], jnp.concatenate([d_summed, act.astype(BF)], axis=0))
        d_r2 = jnp.sum(both[:NB] * tilt, axis=0, keepdims=True)
        readout = both[NB : NB + 1] + both[NB + 1 : NB + 2]
        for k, (s, g) in enumerate(where):
            cut = [slice(j * CELL, (j + 1) * CELL) for j in range(k * UNIT, (k + 1) * UNIT)]
            at = pl.ds(pl.multiple_of(g * UNIT, UNIT), UNIT)
            slope_sum[s, at, :] = jnp.concatenate([d_r2[:, c] for c in cut], axis=0)
            read_sum[s, at, :] = jnp.concatenate([readout[:, c] for c in cut], axis=0)

    def spread(s, g):
        where = [(s, g)]
        while len(where) < UNITS:
            s, g = after(*where[-1])
            where.append((jnp.minimum(s, picked), jnp.where(s < picked, g, 0)))
        return where

    last_tile = jnp.maximum(picked - 1, 0)

    def begin(where):
        r2, half_v, tilt_v = enter(where)
        near_rows[...] = r2
        half_s[...] = half_v
        tilt_s[...] = tilt_v

    def edges(_, here):
        where = spread(*here)
        r2, half_v, tilt_v = near_rows[...], half_s[...], tilt_s[...]
        s, g = after(*where[-1])
        nxt = spread(jnp.minimum(s, picked), jnp.where(s < picked, g, 0))
        rest(where, r2, half_v, tilt_v)
        begin(nxt)
        return nxt[0]

    begin(spread(jnp.int32(0), jnp.int32(0)))
    lax.fori_loop(0, (units + UNITS - 1) // UNITS, edges, (jnp.int32(0), jnp.int32(0)))

    row_at = lax.broadcasted_iota(jnp.int32, (CELL, CELL), 0)
    lane_at = lax.broadcasted_iota(jnp.int32, (CELL, CELL), 1)

    def finish(s, _):
        t = tiles[s]
        num_a, num_b = live_a[t], live_b[t]
        swap = num_a > num_b
        rows_p, lanes_p = jnp.where(swap, pb[s], pa[s]), jnp.where(swap, pa[s], pb[s])
        live = (row_at < jnp.minimum(num_a, num_b)) & (lane_at < jnp.maximum(num_a, num_b))
        near = 1.0 - dist[s] / 8.0
        pull = 2.0 * (-4.0 * slope_sum[s] - near * (0.25 / CELL) * read_sum[s])
        pull = jnp.where(live, pull, 0.0)
        high = pull.astype(BF)
        low = (pull - high.astype(F32)).astype(BF)

        def with_ones(places):
            rows = jnp.concatenate([places[0:3], jnp.ones((1, CELL), F32), jnp.zeros((4, CELL), F32)], axis=0)
            rows = rows.astype(BF)
            return jnp.concatenate([rows, rows], axis=1)

        over_lanes = lax.dot_general(
            with_ones(lanes_p), jnp.concatenate([high, low], axis=1), LAST, preferred_element_type=F32
        )
        over_rows = dot(with_ones(rows_p), jnp.concatenate([high, low], axis=0))
        grad_r = rows_p * over_lanes[3:4] - over_lanes
        grad_l = lanes_p * over_rows[3:4] - over_rows
        grad_a = jnp.where(swap, grad_l, grad_r)
        grad_b = jnp.where(swap, grad_r, grad_l)
        here = pl.ds(pl.multiple_of(first[t] * CELL, CELL), CELL)
        total[:, here] = total[:, here] + grad_a[0:3]
        there = pl.ds(pl.multiple_of(second[t] % cells * CELL, CELL), CELL)

        def add(sums):
            sums[:, there] = sums[:, there] + grad_b[0:3]

        if stage == 0:
            add(total)
        elif stage == 1:
            pl.when(second[t] < cells)(functools.partial(add, total))
            pl.when(second[t] >= cells)(functools.partial(add, side))
        else:
            side[t] = grad_b
        return 0

    lax.fori_loop(0, picked, finish, 0)


def hand_kernel(wanted, total, side, got, total_out, side_out):
    cells = total.shape[1] // CELL
    total_out[...] = total[...]
    side_out[...] = side[...]
    for slot in range(wanted.shape[0]):
        block = wanted[slot] // cells
        here = pl.ds(pl.multiple_of(wanted[slot] % cells * CELL, CELL), CELL)

        def add(sums, slot=slot, here=here):
            sums[:, here] = sums[:, here] + got[slot][0:3]

        pl.when(block == 2)(functools.partial(add, total_out))
        pl.when(block == 3)(functools.partial(add, side_out))


def last_kernel(total, got, out):
    out[...] = -(total[...] + got[...])


def called(kernel, prefetch, operands, out_shape, scratch=(), work=1.0, name=None, bring=False):
    if bring:
        scratch = [*scratch, *[pltpu.VMEM(x.shape, x.dtype) for x in operands]]
        scratch.append(pltpu.SemaphoreType.DMA((len(operands),)))
    return pl.pallas_call(
        kernel,
        grid_spec=pltpu.PrefetchScalarGridSpec(
            num_scalar_prefetch=len(prefetch),
            grid=(1,),
            in_specs=[pl.BlockSpec(memory_space=pltpu.HBM) if bring else VMEM] * len(operands),
            out_specs=jax.tree.map(lambda _: VMEM, out_shape),
            scratch_shapes=list(scratch),
        ),
        out_shape=out_shape,
        compiler_params=pltpu.CompilerParams(vmem_limit_bytes=(64000000 if bring else 40 << 20)),
        cost_estimate=pl.CostEstimate(flops=int(work * 1e9), bytes_accessed=1 << 20, transcendentals=0),
        name=name,
    )(*prefetch, *operands)


def on_device(
    positions,
    features,
    tile_first,
    tile_second,
    count_first,
    count_second,
    w_first,
    w_second,
    radial_weight,
    mix_weight,
    out_weight,
):
    slots = positions.shape[1]
    count = tile_first.shape[0]
    side_f = shifted(features, 0, 1)
    side_p = shifted(positions, 0, 1)
    asked = shifted(tile_second, -1, 0)

    scalars = (tile_first, tile_second, count_first, count_second)
    weights = (w_first, w_second, radial_weight, mix_weight, out_weight.reshape(1, -1))
    sums = jax.ShapeDtypeStruct((3, slots), F32)
    square = (count + 1, CELL, CELL)
    scratch = [
        pltpu.VMEM((2, CELL, CELL), BF),
        pltpu.VMEM((CELL, CELL), BF),
        pltpu.VMEM((CELL, CELL), BF),
        pltpu.VMEM((CELL, CELL), F32),
        pltpu.VMEM((24, 2 * CELL), BF),
        pltpu.VMEM((ROWS, ROWS * CELL), BF),
        *[pltpu.VMEM(square, F32)] * 5,
        pltpu.VMEM((CELL, CELL), BF),
        *[pltpu.VMEM((count, 8, CELL), F32)] * 2,
        pltpu.VMEM((ROWS, CELL), F32),
        pltpu.VMEM((CELL, ROWS * CELL), F32),
        pltpu.VMEM((NB, ROWS * CELL), F32),
        pltpu.SMEM((count + 1,), jnp.int32),
        pltpu.SMEM((count + 1,), jnp.int32),
    ]

    def tiles(stage, extra, outs, work):
        operands = (features, positions, *extra, *weights)
        return called(
            functools.partial(tile_kernel, stage), scalars, operands, outs, scratch, work,
            f"tiles{stage}", bring=stage == 0,
        )

    (total,) = tiles(0, (), (sums,), 8.0)
    packed = called(
        pack_kernel,
        (asked,),
        (features, positions, side_f, side_p),
        jax.ShapeDtypeStruct((count * PACKED, CELL), BF),
        name="pack",
    )
    upper_cells = shifted(packed, 1, 0)
    total, side = tiles(1, (side_f, side_p, total), (sums, sums), 8.0)
    grads = jax.ShapeDtypeStruct((count, 8, CELL), F32)
    total, grads = tiles(2, (upper_cells, total), (sums, grads), 16.0)
    from_upper = shifted(grads, -1, 0)
    total, side = called(hand_kernel, (asked,), (total, side, from_upper), (sums, sums), name="hand")
    from_side = shifted(side, 0, -1)
    return called(last_kernel, (), (total, from_side), sums, name="last")


def solution(mesh):
    whole = ("grp", "dev")
    in_specs = (P(None, whole), P(whole, None), *[P(whole)] * 4, *[P()] * 5)
    return jax.shard_map(
        on_device, mesh=mesh, in_specs=in_specs, out_specs=P(None, whole), check_vma=False
    )
```

```python
import functools

import jax
import jax.numpy as jnp
from jax import lax
from jax.experimental import pallas as pl
from jax.experimental.pallas import tpu as pltpu
from jax.sharding import PartitionSpec as P

CELL = 128
NB = 16
UNIT = 8
UNITS = 2
ROWS = UNIT * UNITS
PACKED = CELL + 16
EARLY = 16
F32, BF = jnp.float32, jnp.bfloat16
LAST = (((1,), (1,)), ((), ()))
VMEM = pl.BlockSpec(memory_space=pltpu.VMEM)


def shifted(array, groups, members):
    n_grp, n_dev = lax.axis_size("grp"), lax.axis_size("dev")
    if groups == 0:
        return lax.ppermute(array, "dev", [(i, (i + members) % n_dev) for i in range(n_dev)])
    if members == 0:
        return lax.ppermute(array, "grp", [(i, (i + groups) % n_grp) for i in range(n_grp)])
    pairs = [
        (g * n_dev + d, (g + groups) % n_grp * n_dev + (d + members) % n_dev)
        for g in range(n_grp)
        for d in range(n_dev)
    ]
    return lax.ppermute(array, ("grp", "dev"), pairs)


def dot(a, b):
    return jnp.dot(a, b, preferred_element_type=F32)


def cell_at(ref, cell):
    return ref[pl.ds(pl.multiple_of(cell * CELL, CELL), CELL), :]


def place_at(ref, cell):
    return ref[:, pl.ds(pl.multiple_of(cell * CELL, CELL), CELL)]


def tall(places):
    return jnp.concatenate([places.astype(F32), jnp.zeros((5, CELL), F32)], axis=0)


def pack_kernel(wanted, _, own_f, own_p, side_f, side_p, out):
    cells = own_f.shape[0] // CELL
    for slot in range(wanted.shape[0]):
        block, cell = wanted[slot] // cells, wanted[slot] % cells

        def put(feats, places, slot=slot, cell=cell):
            base = slot * PACKED
            out[base : base + CELL, :] = cell_at(feats, cell)
            rows = jnp.concatenate([tall(place_at(places, cell)), jnp.zeros((8, CELL), F32)], axis=0)
            out[base + CELL : base + PACKED, :] = rows.astype(BF)

        pl.when(block == 2)(functools.partial(put, own_f, own_p))
        pl.when(block == 3)(functools.partial(put, side_f, side_p))


def tile_kernel(
    stage, first, second, live_a, live_b, own_f, own_p, *refs
):
    extra = (0, 3, 2)[stage]
    remote, refs = refs[:extra], refs[extra:]
    outs = (1, 2, 2)[stage]
    (w_a, w_b, radial, mix, out_w), refs = refs[:5], refs[5:]
    total, side = refs[0], refs[outs - 1]
    refs = refs[outs:]
    if stage == 0:
        given = (own_f, own_p, w_a, w_b, radial, mix, out_w)
        own_f, own_p, w_a, w_b, radial, mix, out_w = held = refs[-8:-1]
        copies = [pltpu.make_async_copy(*pair, refs[-1].at[k]) for k, pair in enumerate(zip(given, held))]
        for copy in copies:
            copy.start()
        for copy in copies:
            copy.wait()
        refs = refs[:-8]
    (
     flip, mix_t, mix_o, scale_o, last, onehot, proj_r, proj_l, dist, slope_sum, read_sum, fb, pa, pb, near_rows, half_s, tilt_s, tiles, steps) = refs
    cells = own_f.shape[0] // CELL
    count = first.shape[0]
    width = ROWS * CELL

    flip[0] = jnp.transpose(w_a[...].astype(F32)).astype(BF)
    flip[1] = jnp.transpose(w_b[...].astype(F32)).astype(BF)
    mix_f = mix[...].astype(F32)
    mix_t[...] = (jnp.transpose(mix_f) * 0.5).astype(BF)
    mix_o[...] = (mix_f * 0.25).astype(BF)
    scale_o[...] = jnp.transpose(jnp.broadcast_to(out_w[...] / CELL, (CELL, CELL)))
    high = out_w[...].astype(BF)
    low = (out_w[...] - high.astype(F32)).astype(BF)
    pad = jnp.zeros((6, CELL), F32)
    left = jnp.concatenate([radial[...].astype(F32), jnp.zeros((8, CELL), F32)], axis=0)
    right = jnp.concatenate([jnp.zeros((NB, CELL), F32), high.astype(F32), low.astype(F32), pad], axis=0)
    last[...] = jnp.concatenate([left, right], axis=1).astype(BF)
    radial_h = radial[...].astype(F32) * 0.5
    row_of = lax.broadcasted_iota(jnp.int32, (ROWS, width), 0)
    lane_of = lax.broadcasted_iota(jnp.int32, (ROWS, width), 1) // CELL
    onehot[...] = jnp.where(row_of == lane_of, 1.0, 0.0).astype(BF)
    centers = lax.broadcasted_iota(jnp.int32, (NB, CELL), 0).astype(F32) * (6.75 / NB)

    if stage == 0:
        total[...] = jnp.zeros_like(total)
    else:
        total[...] = remote[-1][...]
    if stage == 1:
        side[...] = jnp.zeros_like(side)

    picked, early = jnp.int32(0), jnp.int32(0)
    for t in range(count):
        block = second[t] // cells
        need = (jnp.minimum(live_a[t], live_b[t]) + UNIT - 1) // UNIT
        soon = (block == 0) & (early + need <= EARLY)
        early = early + jnp.where(soon, need, 0)
        take = (soon, (block < 2) & ~soon, block >= 2)[stage]
        tiles[picked] = jnp.int32(t)
        picked = picked + take.astype(jnp.int32)

    def prepare(s, so_far):
        t = tiles[s]
        cell = second[t] % cells
        pa[s] = tall(place_at(own_p, first[t]))
        if stage == 2:
            base = pl.multiple_of(t * PACKED, 16)
            fb[...] = remote[0][pl.ds(base, CELL), :]
            rest = remote[0][pl.ds(pl.multiple_of(base + CELL, 16), 16), :]
            pb[s] = rest.astype(F32)[0:8]
        else:
            def bring(feats, places):
                fb[...] = cell_at(feats, cell)
                pb[s] = tall(place_at(places, cell))

            if stage == 0:
                bring(own_f, own_p)
            else:
                pl.when(second[t] < cells)(functools.partial(bring, own_f, own_p))
                pl.when(second[t] >= cells)(functools.partial(bring, remote[0], remote[1]))
        num_a, num_b = live_a[t], live_b[t]
        swap = num_a > num_b
        feats_a, feats_b = cell_at(own_f, first[t]), fb[...]
        rows_f = jnp.where(swap, feats_b, feats_a)
        lanes_f = jnp.where(swap, feats_a, feats_b)
        rows_p, lanes_p = jnp.where(swap, pb[s], pa[s]), jnp.where(swap, pa[s], pb[s])
        w_r = jnp.where(swap, w_b[...], w_a[...])
        w_l = jnp.where(swap, flip[0], flip[1])
        proj_r[s] = dot(rows_f, w_r).astype(BF).astype(F32) * 0.5
        proj_l[s] = lax.dot_general(w_l, lanes_f, LAST, preferred_element_type=F32).astype(BF).astype(F32) * 0.5
        tall_p = jnp.transpose(rows_p)
        gaps = [tall_p[:, c : c + 1] - lanes_p[c : c + 1, :] for c in range(3)]
        dist[s] = gaps[0] * gaps[0] + gaps[1] * gaps[1] + gaps[2] * gaps[2]
        n = (jnp.minimum(num_a, num_b) + UNIT - 1) // UNIT
        steps[s] = n
        return so_far + n

    units = lax.fori_loop(0, picked, prepare, jnp.int32(0))

    proj_r[picked, 0:UNIT, :] = jnp.zeros((UNIT, CELL), F32)
    dist[picked, 0:UNIT, :] = jnp.zeros((UNIT, CELL), F32)

    def after(s, g):
        over = g + 1 >= steps[s]
        return jnp.where(over, s + 1, s), jnp.where(over, 0, g + 1)

    def rows_of(ref, where):
        return [ref[s, pl.ds(pl.multiple_of(g * UNIT, UNIT), UNIT), :] for s, g in where]

    def enter(where):
        r2 = jnp.concatenate(rows_of(dist, where), axis=0)
        weights = jnp.transpose(jnp.concatenate([radial_h, *rows_of(proj_r, where)], axis=0)).astype(BF)
        offset = jnp.concatenate(
            [jnp.broadcast_to(r2[k : k + 1, :], (NB, CELL)) - centers for k in range(ROWS)], axis=1
        )
        basis = jnp.exp(-2.0 * offset * offset)
        inputs = jnp.concatenate([basis.astype(BF), onehot[...]], axis=0)
        lanes = jnp.concatenate([proj_l[s] for s, g in where for _ in range(UNIT)], axis=1)
        return r2, dot(weights, inputs) + lanes, basis * offset

    def rest(where, r2, half, tilt):
        bend = jnp.tanh(half)
        up = 1 + bend
        latent = half * up
        slope = up + latent * (1 - bend)
        pre = dot(mix_t[...], latent.astype(BF))
        bend = jnp.tanh(pre)
        up = 1 + bend
        act = pre * up
        near = 1.0 - r2 / 8.0
        near = near * near
        envelope = jnp.concatenate([near[k : k + 1, :] for k in range(ROWS)], axis=1)
        d_pre = envelope * jnp.concatenate([scale_o[...]] * ROWS, axis=1) * (up + act * (1 - bend))
        d_latent = dot(mix_o[...], d_pre.astype(BF))
        d_summed = (d_latent * slope).astype(BF)
        both = dot(last[...], jnp.concatenate([d_summed, act.astype(BF)], axis=0))
        d_r2 = jnp.sum(both[:NB] * tilt, axis=0, keepdims=True)
        readout = both[NB : NB + 1] + both[NB + 1 : NB + 2]
        for k, (s, g) in enumerate(where):
            cut = [slice(j * CELL, (j + 1) * CELL) for j in range(k * UNIT, (k + 1) * UNIT)]
            at = pl.ds(pl.multiple_of(g * UNIT, UNIT), UNIT)
            slope_sum[s, at, :] = jnp.concatenate([d_r2[:, c] for c in cut], axis=0)
            read_sum[s, at, :] = jnp.concatenate([readout[:, c] for c in cut], axis=0)

    def spread(s, g):
        where = [(s, g)]
        while len(where) < UNITS:
            s, g = after(*where[-1])
            where.append((jnp.minimum(s, picked), jnp.where(s < picked, g, 0)))
        return where

    last_tile = jnp.maximum(picked - 1, 0)

    def begin(where):
        r2, half_v, tilt_v = enter(where)
        near_rows[...] = r2
        half_s[...] = half_v
        tilt_s[...] = tilt_v

    def edges(_, here):
        where = spread(*here)
        r2, half_v, tilt_v = near_rows[...], half_s[...], tilt_s[...]
        s, g = after(*where[-1])
        nxt = spread(jnp.minimum(s, picked), jnp.where(s < picked, g, 0))
        rest(where, r2, half_v, tilt_v)
        begin(nxt)
        return nxt[0]

    begin(spread(jnp.int32(0), jnp.int32(0)))
    lax.fori_loop(0, (units + UNITS - 1) // UNITS, edges, (jnp.int32(0), jnp.int32(0)))

    row_at = lax.broadcasted_iota(jnp.int32, (CELL, CELL), 0)
    lane_at = lax.broadcasted_iota(jnp.int32, (CELL, CELL), 1)

    def finish(s, _):
        t = tiles[s]
        num_a, num_b = live_a[t], live_b[t]
        swap = num_a > num_b
        rows_p, lanes_p = jnp.where(swap, pb[s], pa[s]), jnp.where(swap, pa[s], pb[s])
        live = (row_at < jnp.minimum(num_a, num_b)) & (lane_at < jnp.maximum(num_a, num_b))
        near = 1.0 - dist[s] / 8.0
        pull = 2.0 * (-4.0 * slope_sum[s] - near * (0.25 / CELL) * read_sum[s])
        pull = jnp.where(live, pull, 0.0)
        high = pull.astype(BF)
        low = (pull - high.astype(F32)).astype(BF)

        def with_ones(places):
            rows = jnp.concatenate([places[0:3], jnp.ones((1, CELL), F32), jnp.zeros((4, CELL), F32)], axis=0)
            rows = rows.astype(BF)
            return jnp.concatenate([rows, rows], axis=1)

        over_lanes = lax.dot_general(
            with_ones(lanes_p), jnp.concatenate([high, low], axis=1), LAST, preferred_element_type=F32
        )
        over_rows = dot(with_ones(rows_p), jnp.concatenate([high, low], axis=0))
        grad_r = rows_p * over_lanes[3:4] - over_lanes
        grad_l = lanes_p * over_rows[3:4] - over_rows
        grad_a = jnp.where(swap, grad_l, grad_r)
        grad_b = jnp.where(swap, grad_r, grad_l)
        here = pl.ds(pl.multiple_of(first[t] * CELL, CELL), CELL)
        total[:, here] = total[:, here] + grad_a[0:3]
        there = pl.ds(pl.multiple_of(second[t] % cells * CELL, CELL), CELL)

        def add(sums):
            sums[:, there] = sums[:, there] + grad_b[0:3]

        if stage == 0:
            add(total)
        elif stage == 1:
            pl.when(second[t] < cells)(functools.partial(add, total))
            pl.when(second[t] >= cells)(functools.partial(add, side))
        else:
            side[t] = grad_b
        return 0

    lax.fori_loop(0, picked, finish, 0)


def last_kernel(wanted, wanted_far, total, upper, corner, side, out):
    cells = total.shape[1] // CELL
    out[...] = -(total[...] + side[...])
    for slot in range(wanted.shape[0]):
        for asked, block, got in ((wanted, 2, upper), (wanted_far, 3, corner)):

            @pl.when(asked[slot] // cells == block)
            def _(asked=asked, got=got, slot=slot):
                here = pl.ds(pl.multiple_of(asked[slot] % cells * CELL, CELL), CELL)
                out[:, here] = out[:, here] - got[slot][0:3]


def called(kernel, prefetch, operands, out_shape, scratch=(), work=1.0, name=None, bring=False):
    if bring:
        scratch = [*scratch, *[pltpu.VMEM(x.shape, x.dtype) for x in operands]]
        scratch.append(pltpu.SemaphoreType.DMA((len(operands),)))
    return pl.pallas_call(
        kernel,
        grid_spec=pltpu.PrefetchScalarGridSpec(
            num_scalar_prefetch=len(prefetch),
            grid=(1,),
            in_specs=[pl.BlockSpec(memory_space=pltpu.HBM) if bring else VMEM] * len(operands),
            out_specs=jax.tree.map(lambda _: VMEM, out_shape),
            scratch_shapes=list(scratch),
        ),
        out_shape=out_shape,
        compiler_params=pltpu.CompilerParams(vmem_limit_bytes=(64000000 if bring else 40 << 20)),
        cost_estimate=pl.CostEstimate(flops=int(work * 1e9), bytes_accessed=1 << 20, transcendentals=0),
        name=name,
    )(*prefetch, *operands)


def on_device(
    positions,
    features,
    tile_first,
    tile_second,
    count_first,
    count_second,
    w_first,
    w_second,
    radial_weight,
    mix_weight,
    out_weight,
):
    slots = positions.shape[1]
    count = tile_first.shape[0]
    side_f = shifted(features, 0, 1)
    side_p = shifted(positions, 0, 1)
    asked = shifted(tile_second, -1, 0)
    asked_far = shifted(tile_second, -1, -1)

    scalars = (tile_first, tile_second, count_first, count_second)
    weights = (w_first, w_second, radial_weight, mix_weight, out_weight.reshape(1, -1))
    sums = jax.ShapeDtypeStruct((3, slots), F32)
    square = (count + 1, CELL, CELL)
    scratch = [
        pltpu.VMEM((2, CELL, CELL), BF),
        pltpu.VMEM((CELL, CELL), BF),
        pltpu.VMEM((CELL, CELL), BF),
        pltpu.VMEM((CELL, CELL), F32),
        pltpu.VMEM((24, 2 * CELL), BF),
        pltpu.VMEM((ROWS, ROWS * CELL), BF),
        *[pltpu.VMEM(square, F32)] * 5,
        pltpu.VMEM((CELL, CELL), BF),
        *[pltpu.VMEM((count, 8, CELL), F32)] * 2,
        pltpu.VMEM((ROWS, CELL), F32),
        pltpu.VMEM((CELL, ROWS * CELL), F32),
        pltpu.VMEM((NB, ROWS * CELL), F32),
        pltpu.SMEM((count + 1,), jnp.int32),
        pltpu.SMEM((count + 1,), jnp.int32),
    ]

    def tiles(stage, extra, outs, work):
        operands = (features, positions, *extra, *weights)
        return called(
            functools.partial(tile_kernel, stage), scalars, operands, outs, scratch, work,
            f"tiles{stage}", bring=stage == 0,
        )

    (total,) = tiles(0, (), (sums,), 8.0)
    packed = called(
        pack_kernel,
        (asked, asked_far),
        (features, positions, side_f, side_p),
        jax.ShapeDtypeStruct((count * PACKED, CELL), BF),
        name="pack",
    )
    upper_cells = shifted(packed, 1, 0)
    total, side = tiles(1, (side_f, side_p, total), (sums, sums), 8.0)
    grads = jax.ShapeDtypeStruct((count, 8, CELL), F32)
    total, grads = tiles(2, (upper_cells, total), (sums, grads), 16.0)
    from_upper = shifted(grads, -1, 0)
    from_corner = shifted(grads, -1, -1)
    side, _ = lax.optimization_barrier((side, grads))
    from_side = shifted(side, 0, -1)
    return called(
        last_kernel, (asked, asked_far), (total, from_upper, from_corner, from_side), sums, name="last"
    )


def solution(mesh):
    whole = ("grp", "dev")
    in_specs = (P(None, whole), P(whole, None), *[P(whole)] * 4, *[P()] * 5)
    return jax.shard_map(
        on_device, mesh=mesh, in_specs=in_specs, out_specs=P(None, whole), check_vma=False
    )
```

```python
import functools

import jax
import jax.numpy as jnp
from jax import lax
from jax.experimental import pallas as pl
from jax.experimental.pallas import tpu as pltpu
from jax.sharding import PartitionSpec as P

CELL = 128
NB = 16
UNIT = 8
UNITS = 2
ROWS = UNIT * UNITS
PACKED = CELL + 16
EARLY = 16
F32, BF = jnp.float32, jnp.bfloat16
LAST = (((1,), (1,)), ((), ()))
VMEM = pl.BlockSpec(memory_space=pltpu.VMEM)


def shifted(array, groups, members):
    n_grp, n_dev = lax.axis_size("grp"), lax.axis_size("dev")
    if groups == 0:
        return lax.ppermute(array, "dev", [(i, (i + members) % n_dev) for i in range(n_dev)])
    if members == 0:
        return lax.ppermute(array, "grp", [(i, (i + groups) % n_grp) for i in range(n_grp)])
    pairs = [
        (g * n_dev + d, (g + groups) % n_grp * n_dev + (d + members) % n_dev)
        for g in range(n_grp)
        for d in range(n_dev)
    ]
    return lax.ppermute(array, ("grp", "dev"), pairs)


def dot(a, b):
    return jnp.dot(a, b, preferred_element_type=F32)


def cell_at(ref, cell):
    return ref[pl.ds(pl.multiple_of(cell * CELL, CELL), CELL), :]


def place_at(ref, cell):
    return ref[:, pl.ds(pl.multiple_of(cell * CELL, CELL), CELL)]


def tall(places):
    return jnp.concatenate([places.astype(F32), jnp.zeros((5, CELL), F32)], axis=0)


def pack_kernel(wanted, _, own_f, own_p, side_f, side_p, out):
    cells = own_f.shape[0] // CELL
    for slot in range(wanted.shape[0]):
        block, cell = wanted[slot] // cells, wanted[slot] % cells

        def put(feats, places, slot=slot, cell=cell):
            base = slot * PACKED
            out[base : base + CELL, :] = cell_at(feats, cell)
            rows = jnp.concatenate([tall(place_at(places, cell)), jnp.zeros((8, CELL), F32)], axis=0)
            out[base + CELL : base + PACKED, :] = rows.astype(BF)

        pl.when(block == 2)(functools.partial(put, own_f, own_p))
        pl.when(block == 3)(functools.partial(put, side_f, side_p))


def units_of(rows, lanes):
    thirds = rows // 32 * 3 + jnp.minimum(3, (rows % 32 + 7) // 8)
    return jnp.where(lanes > 96, (rows + 7) // 8, jnp.where(lanes > 64, thirds, (rows + 15) // 16))


def kind_of(lanes):
    return jnp.where(lanes > 96, 0, jnp.where(lanes > 64, 1, 2))


def folded(kind, rows, lane_at):
    eight = [rows[k : k + 8] for k in range(0, CELL, 8)]
    out = []
    if kind == 1:
        for q in range(0, 16, 4):
            for u in range(3):
                moved = pltpu.roll(eight[q + 3], 96 - 32 * u, 1)
                out.append(jnp.where(lane_at[:8] < 96, eight[q + u], moved))
    else:
        for q in range(0, 8, 2):
            out.append(jnp.where(lane_at[:8] < 64, eight[q], pltpu.roll(eight[q + 1], 64, 1)))
    return jnp.concatenate(out, axis=0)


def unfolded(kind, rows, lane_at):
    eight = [rows[k : k + 8] for k in range(0, CELL, 8)]
    out = []
    if kind == 1:
        for q in range(0, 12, 3):
            out.extend(eight[q : q + 3])
            first, second, third = (pltpu.roll(eight[q + u], 32 * u + 32, 1) for u in range(3))
            out.append(jnp.where(lane_at[:8] < 32, first, jnp.where(lane_at[:8] < 64, second, third)))
    else:
        for q in range(4):
            out.extend((eight[q], pltpu.roll(eight[q], 64, 1)))
        out.extend(eight[8:])
    return jnp.concatenate(out, axis=0)


def tile_kernel(
    stage, first, second, live_a, live_b, own_f, own_p, *refs
):
    extra = (0, 3, 2)[stage]
    remote, refs = refs[:extra], refs[extra:]
    outs = (1, 2, 2)[stage]
    (w_a, w_b, radial, mix, out_w), refs = refs[:5], refs[5:]
    total, side = refs[0], refs[outs - 1]
    refs = refs[outs:]
    if stage == 0:
        given = (own_f, own_p, w_a, w_b, radial, mix, out_w)
        own_f, own_p, w_a, w_b, radial, mix, out_w = held = refs[-8:-1]
        copies = [pltpu.make_async_copy(*pair, refs[-1].at[k]) for k, pair in enumerate(zip(given, held))]
        for copy in copies:
            copy.start()
        for copy in copies:
            copy.wait()
        refs = refs[:-8]
    (
     flip, mix_t, mix_o, scale_o, last, onehot, proj_r, plain, dist, slope_sum, read_sum, proj_l, fb, pa, pb, near_rows, half_s, tilt_s, tiles, steps, kinds) = refs
    cells = own_f.shape[0] // CELL
    count = first.shape[0]

    flip[0] = jnp.transpose(w_a[...].astype(F32)).astype(BF)
    flip[1] = jnp.transpose(w_b[...].astype(F32)).astype(BF)
    mix_f = mix[...].astype(F32)
    mix_t[...] = (jnp.transpose(mix_f) * 0.5).astype(BF)
    mix_o[...] = (mix_f * 0.25).astype(BF)
    scale_o[...] = jnp.transpose(jnp.broadcast_to(out_w[...] / CELL, (CELL, CELL)))
    high = out_w[...].astype(BF)
    low = (out_w[...] - high.astype(F32)).astype(BF)
    pad = jnp.zeros((6, CELL), F32)
    left = jnp.concatenate([radial[...].astype(F32), jnp.zeros((8, CELL), F32)], axis=0)
    right = jnp.concatenate([jnp.zeros((NB, CELL), F32), high.astype(F32), low.astype(F32), pad], axis=0)
    last[...] = jnp.concatenate([left, right], axis=1).astype(BF)
    radial_h = radial[...].astype(F32) * 0.5
    row_of = lax.broadcasted_iota(jnp.int32, (2 * UNIT, UNIT * CELL), 0)
    at_lane = lax.broadcasted_iota(jnp.int32, (2 * UNIT, UNIT * CELL), 1)
    for kind, bound in enumerate((128, 96, 64)):
        held_row = at_lane // CELL + jnp.where(at_lane % CELL < bound, 0, UNIT)
        onehot[kind] = jnp.where(row_of == held_row, 1.0, 0.0).astype(BF)
    row_at = lax.broadcasted_iota(jnp.int32, (CELL, CELL), 0)
    lane_at = lax.broadcasted_iota(jnp.int32, (CELL, CELL), 1)
    centers = lax.broadcasted_iota(jnp.int32, (NB, CELL), 0).astype(F32) * (6.75 / NB)

    if stage == 0:
        total[...] = jnp.zeros_like(total)
    else:
        total[...] = remote[-1][...]
    if stage == 1:
        side[...] = jnp.zeros_like(side)

    picked, early = jnp.int32(0), jnp.int32(0)
    for t in range(count):
        block = second[t] // cells
        need = units_of(jnp.minimum(live_a[t], live_b[t]), jnp.maximum(live_a[t], live_b[t]))
        soon = (block == 0) & (early + need <= EARLY)
        early = early + jnp.where(soon, need, 0)
        take = (soon, (block < 2) & ~soon, block >= 2)[stage]
        tiles[picked] = jnp.int32(t)
        picked = picked + take.astype(jnp.int32)

    def prepare(s, so_far):
        t = tiles[s]
        cell = second[t] % cells
        pa[s] = tall(place_at(own_p, first[t]))
        if stage == 2:
            base = pl.multiple_of(t * PACKED, 16)
            fb[...] = remote[0][pl.ds(base, CELL), :]
            rest = remote[0][pl.ds(pl.multiple_of(base + CELL, 16), 16), :]
            pb[s] = rest.astype(F32)[0:8]
        else:
            def bring(feats, places):
                fb[...] = cell_at(feats, cell)
                pb[s] = tall(place_at(places, cell))

            if stage == 0:
                bring(own_f, own_p)
            else:
                pl.when(second[t] < cells)(functools.partial(bring, own_f, own_p))
                pl.when(second[t] >= cells)(functools.partial(bring, remote[0], remote[1]))
        num_a, num_b = live_a[t], live_b[t]
        swap = num_a > num_b
        feats_a, feats_b = cell_at(own_f, first[t]), fb[...]
        rows_f = jnp.where(swap, feats_b, feats_a)
        lanes_f = jnp.where(swap, feats_a, feats_b)
        rows_p, lanes_p = jnp.where(swap, pb[s], pa[s]), jnp.where(swap, pa[s], pb[s])
        w_r = jnp.where(swap, w_b[...], w_a[...])
        w_l = jnp.where(swap, flip[0], flip[1])
        proj_r[s] = dot(rows_f, w_r).astype(BF).astype(F32) * 0.5
        lane_proj = lax.dot_general(w_l, lanes_f, LAST, preferred_element_type=F32).astype(BF).astype(F32) * 0.5
        tall_p = jnp.transpose(rows_p)
        gaps = [tall_p[:, c : c + 1] - lanes_p[c : c + 1, :] for c in range(3)]
        r2 = gaps[0] * gaps[0] + gaps[1] * gaps[1] + gaps[2] * gaps[2]
        plain[s] = r2
        lanes = jnp.maximum(num_a, num_b)
        kind = kind_of(lanes)

        @pl.when(kind == 0)
        def _():
            dist[s] = r2
            proj_l[s, 0] = lane_proj

        @pl.when(kind == 1)
        def _():
            dist[s, 0:96, :] = folded(1, r2, lane_at)
            for u in range(3):
                proj_l[s, u] = jnp.where(lane_at < 96, lane_proj, pltpu.roll(lane_proj, 96 - 32 * u, 1))

        @pl.when(kind == 2)
        def _():
            dist[s, 0:32, :] = folded(2, r2, lane_at)
            proj_l[s, 0] = jnp.where(lane_at < 64, lane_proj, pltpu.roll(lane_proj, 64, 1))

        kinds[s] = kind
        n = units_of(jnp.minimum(num_a, num_b), lanes)
        steps[s] = n
        return so_far + n

    units = lax.fori_loop(0, picked, prepare, jnp.int32(0))

    proj_r[picked, 0:UNIT, :] = jnp.zeros((UNIT, CELL), F32)
    dist[picked, 0:UNIT, :] = jnp.zeros((UNIT, CELL), F32)
    kinds[picked] = jnp.int32(0)

    def after(s, g):
        over = g + 1 >= steps[s]
        return jnp.where(over, s + 1, s), jnp.where(over, 0, g + 1)

    def rows_of(ref, where):
        return [ref[s, pl.ds(pl.multiple_of(g * UNIT, UNIT), UNIT), :] for s, g in where]

    def enter(where):
        r2 = jnp.concatenate(rows_of(dist, where), axis=0)
        firsts, ones, lanes = [], [], []
        for k, (s, g) in enumerate(where):
            kind = kinds[s]
            third, part = g // 3, g % 3
            main = jnp.where(kind == 0, UNIT * g, jnp.where(kind == 1, 32 * third + UNIT * part, 2 * UNIT * g))
            more = jnp.where(kind == 0, UNIT * g, jnp.where(kind == 1, 32 * third + 3 * UNIT, 2 * UNIT * g + UNIT))
            for base in (main, more):
                firsts.append(proj_r[s, pl.ds(pl.multiple_of(base, UNIT), UNIT), :])
            blank = jnp.zeros((2 * UNIT, UNIT * CELL), BF)
            ones.append(jnp.concatenate([onehot[kind] if j == k else blank for j in range(UNITS)], axis=1))
            lanes.extend([proj_l[s, jnp.where(kind == 1, part, 0)]] * UNIT)
        weights = jnp.transpose(jnp.concatenate([radial_h, *firsts], axis=0)).astype(BF)
        offset = jnp.concatenate(
            [jnp.broadcast_to(r2[k : k + 1, :], (NB, CELL)) - centers for k in range(ROWS)], axis=1
        )
        basis = jnp.exp(-2.0 * offset * offset)
        inputs = jnp.concatenate([basis.astype(BF), *ones], axis=0)
        return r2, dot(weights, inputs) + jnp.concatenate(lanes, axis=1), basis * offset

    def rest(where, r2, half, tilt):
        bend = jnp.tanh(half)
        up = 1 + bend
        latent = half * up
        slope = up + latent * (1 - bend)
        pre = dot(mix_t[...], latent.astype(BF))
        bend = jnp.tanh(pre)
        up = 1 + bend
        act = pre * up
        near = 1.0 - r2 / 8.0
        near = near * near
        envelope = jnp.concatenate([near[k : k + 1, :] for k in range(ROWS)], axis=1)
        d_pre = envelope * jnp.concatenate([scale_o[...]] * ROWS, axis=1) * (up + act * (1 - bend))
        d_latent = dot(mix_o[...], d_pre.astype(BF))
        d_summed = (d_latent * slope).astype(BF)
        both = dot(last[...], jnp.concatenate([d_summed, act.astype(BF)], axis=0))
        d_r2 = jnp.sum(both[:NB] * tilt, axis=0, keepdims=True)
        readout = both[NB : NB + 1] + both[NB + 1 : NB + 2]
        for k, (s, g) in enumerate(where):
            cut = [slice(j * CELL, (j + 1) * CELL) for j in range(k * UNIT, (k + 1) * UNIT)]
            at = pl.ds(pl.multiple_of(g * UNIT, UNIT), UNIT)
            slope_sum[s, at, :] = jnp.concatenate([d_r2[:, c] for c in cut], axis=0)
            read_sum[s, at, :] = jnp.concatenate([readout[:, c] for c in cut], axis=0)

    def spread(s, g):
        where = [(s, g)]
        while len(where) < UNITS:
            s, g = after(*where[-1])
            where.append((jnp.minimum(s, picked), jnp.where(s < picked, g, 0)))
        return where

    last_tile = jnp.maximum(picked - 1, 0)

    def begin(where):
        r2, half_v, tilt_v = enter(where)
        near_rows[...] = r2
        half_s[...] = half_v
        tilt_s[...] = tilt_v

    def edges(_, here):
        where = spread(*here)
        r2, half_v, tilt_v = near_rows[...], half_s[...], tilt_s[...]
        s, g = after(*where[-1])
        nxt = spread(jnp.minimum(s, picked), jnp.where(s < picked, g, 0))
        rest(where, r2, half_v, tilt_v)
        begin(nxt)
        return nxt[0]

    begin(spread(jnp.int32(0), jnp.int32(0)))
    lax.fori_loop(0, (units + UNITS - 1) // UNITS, edges, (jnp.int32(0), jnp.int32(0)))

    def finish(s, _):
        t = tiles[s]
        num_a, num_b = live_a[t], live_b[t]
        swap = num_a > num_b
        rows_p, lanes_p = jnp.where(swap, pb[s], pa[s]), jnp.where(swap, pa[s], pb[s])
        live = (row_at < jnp.minimum(num_a, num_b)) & (lane_at < jnp.maximum(num_a, num_b))
        for kind in (1, 2):

            @pl.when(kinds[s] == kind)
            def _(kind=kind):
                slope_sum[s] = unfolded(kind, slope_sum[s], lane_at)
                read_sum[s] = unfolded(kind, read_sum[s], lane_at)

        near = 1.0 - plain[s] / 8.0
        pull = 2.0 * (-4.0 * slope_sum[s] - near * (0.25 / CELL) * read_sum[s])
        pull = jnp.where(live, pull, 0.0)
        high = pull.astype(BF)
        low = (pull - high.astype(F32)).astype(BF)

        def with_ones(places):
            rows = jnp.concatenate([places[0:3], jnp.ones((1, CELL), F32), jnp.zeros((4, CELL), F32)], axis=0)
            rows = rows.astype(BF)
            return jnp.concatenate([rows, rows], axis=1)

        over_lanes = lax.dot_general(
            with_ones(lanes_p), jnp.concatenate([high, low], axis=1), LAST, preferred_element_type=F32
        )
        over_rows = dot(with_ones(rows_p), jnp.concatenate([high, low], axis=0))
        grad_r = rows_p * over_lanes[3:4] - over_lanes
        grad_l = lanes_p * over_rows[3:4] - over_rows
        grad_a = jnp.where(swap, grad_l, grad_r)
        grad_b = jnp.where(swap, grad_r, grad_l)
        here = pl.ds(pl.multiple_of(first[t] * CELL, CELL), CELL)
        total[:, here] = total[:, here] + grad_a[0:3]
        there = pl.ds(pl.multiple_of(second[t] % cells * CELL, CELL), CELL)

        def add(sums):
            sums[:, there] = sums[:, there] + grad_b[0:3]

        if stage == 0:
            add(total)
        elif stage == 1:
            pl.when(second[t] < cells)(functools.partial(add, total))
            pl.when(second[t] >= cells)(functools.partial(add, side))
        else:
            side[t] = grad_b
        return 0

    lax.fori_loop(0, picked, finish, 0)


def last_kernel(wanted, wanted_far, total, upper, corner, side, out):
    cells = total.shape[1] // CELL
    out[...] = -(total[...] + side[...])
    for slot in range(wanted.shape[0]):
        for asked, block, got in ((wanted, 2, upper), (wanted_far, 3, corner)):

            @pl.when(asked[slot] // cells == block)
            def _(asked=asked, got=got, slot=slot):
                here = pl.ds(pl.multiple_of(asked[slot] % cells * CELL, CELL), CELL)
                out[:, here] = out[:, here] - got[slot][0:3]


def called(kernel, prefetch, operands, out_shape, scratch=(), work=1.0, name=None, bring=False):
    if bring:
        scratch = [*scratch, *[pltpu.VMEM(x.shape, x.dtype) for x in operands]]
        scratch.append(pltpu.SemaphoreType.DMA((len(operands),)))
    return pl.pallas_call(
        kernel,
        grid_spec=pltpu.PrefetchScalarGridSpec(
            num_scalar_prefetch=len(prefetch),
            grid=(1,),
            in_specs=[pl.BlockSpec(memory_space=pltpu.HBM) if bring else VMEM] * len(operands),
            out_specs=jax.tree.map(lambda _: VMEM, out_shape),
            scratch_shapes=list(scratch),
        ),
        out_shape=out_shape,
        compiler_params=pltpu.CompilerParams(vmem_limit_bytes=(64000000 if bring else 40 << 20)),
        cost_estimate=pl.CostEstimate(flops=int(work * 1e9), bytes_accessed=1 << 20, transcendentals=0),
        name=name,
    )(*prefetch, *operands)


def on_device(
    positions,
    features,
    tile_first,
    tile_second,
    count_first,
    count_second,
    w_first,
    w_second,
    radial_weight,
    mix_weight,
    out_weight,
):
    slots = positions.shape[1]
    count = tile_first.shape[0]
    side_f = shifted(features, 0, 1)
    side_p = shifted(positions, 0, 1)
    asked = shifted(tile_second, -1, 0)
    asked_far = shifted(tile_second, -1, -1)

    scalars = (tile_first, tile_second, count_first, count_second)
    weights = (w_first, w_second, radial_weight, mix_weight, out_weight.reshape(1, -1))
    sums = jax.ShapeDtypeStruct((3, slots), F32)
    square = (count + 1, CELL, CELL)
    scratch = [
        pltpu.VMEM((2, CELL, CELL), BF),
        pltpu.VMEM((CELL, CELL), BF),
        pltpu.VMEM((CELL, CELL), BF),
        pltpu.VMEM((CELL, CELL), F32),
        pltpu.VMEM((24, 2 * CELL), BF),
        pltpu.VMEM((3, 2 * UNIT, UNIT * CELL), BF),
        *[pltpu.VMEM(square, F32)] * 5,
        pltpu.VMEM((count + 1, 3, CELL, CELL), F32),
        pltpu.VMEM((CELL, CELL), BF),
        *[pltpu.VMEM((count, 8, CELL), F32)] * 2,
        pltpu.VMEM((ROWS, CELL), F32),
        pltpu.VMEM((CELL, ROWS * CELL), F32),
        pltpu.VMEM((NB, ROWS * CELL), F32),
        *[pltpu.SMEM((count + 1,), jnp.int32)] * 3,
    ]

    def tiles(stage, extra, outs, work):
        operands = (features, positions, *extra, *weights)
        return called(
            functools.partial(tile_kernel, stage), scalars, operands, outs, scratch, work,
            f"tiles{stage}", bring=stage == 0,
        )

    (total,) = tiles(0, (), (sums,), 8.0)
    packed = called(
        pack_kernel,
        (asked, asked_far),
        (features, positions, side_f, side_p),
        jax.ShapeDtypeStruct((count * PACKED, CELL), BF),
        name="pack",
    )
    upper_cells = shifted(packed, 1, 0)
    total, side = tiles(1, (side_f, side_p, total), (sums, sums), 8.0)
    grads = jax.ShapeDtypeStruct((count, 8, CELL), F32)
    total, grads = tiles(2, (upper_cells, total), (sums, grads), 16.0)
    from_upper = shifted(grads, -1, 0)
    from_corner = shifted(grads, -1, -1)
    side, _ = lax.optimization_barrier((side, grads))
    from_side = shifted(side, 0, -1)
    return called(
        last_kernel, (asked, asked_far), (total, from_upper, from_corner, from_side), sums, name="last"
    )


def solution(mesh):
    whole = ("grp", "dev")
    in_specs = (P(None, whole), P(whole, None), *[P(whole)] * 4, *[P()] * 5)
    return jax.shard_map(
        on_device, mesh=mesh, in_specs=in_specs, out_specs=P(None, whole), check_vma=False
    )
```

```python
import functools

import jax
import jax.numpy as jnp
from jax import lax
from jax.experimental import pallas as pl
from jax.experimental.pallas import tpu as pltpu
from jax.sharding import PartitionSpec as P

CELL = 128
NB = 16
UNIT = 8
UNITS = 2
ROWS = UNIT * UNITS
PACKED = CELL + 16
EARLY = 16
F32, BF = jnp.float32, jnp.bfloat16
LAST = (((1,), (1,)), ((), ()))
VMEM = pl.BlockSpec(memory_space=pltpu.VMEM)


def shifted(array, groups, members):
    n_grp, n_dev = lax.axis_size("grp"), lax.axis_size("dev")
    if groups == 0:
        return lax.ppermute(array, "dev", [(i, (i + members) % n_dev) for i in range(n_dev)])
    if members == 0:
        return lax.ppermute(array, "grp", [(i, (i + groups) % n_grp) for i in range(n_grp)])
    pairs = [
        (g * n_dev + d, (g + groups) % n_grp * n_dev + (d + members) % n_dev)
        for g in range(n_grp)
        for d in range(n_dev)
    ]
    return lax.ppermute(array, ("grp", "dev"), pairs)


def dot(a, b):
    return jnp.dot(a, b, preferred_element_type=F32)


def cell_at(ref, cell):
    return ref[pl.ds(pl.multiple_of(cell * CELL, CELL), CELL), :]


def place_at(ref, cell):
    return ref[:, pl.ds(pl.multiple_of(cell * CELL, CELL), CELL)]


def tall(places):
    return jnp.concatenate([places.astype(F32), jnp.zeros((5, CELL), F32)], axis=0)


def pack_kernel(wanted, own_f, own_p, side_f, side_p, out):
    cells = own_f.shape[0] // CELL
    for slot in range(wanted.shape[0]):
        block, cell = wanted[slot] // cells, wanted[slot] % cells

        def put(feats, places, slot=slot, cell=cell):
            base = slot * PACKED
            out[base : base + CELL, :] = cell_at(feats, cell)
            rows = jnp.concatenate([tall(place_at(places, cell)), jnp.zeros((8, CELL), F32)], axis=0)
            out[base + CELL : base + PACKED, :] = rows.astype(BF)

        pl.when(block == 2)(functools.partial(put, own_f, own_p))
        pl.when(block == 3)(functools.partial(put, side_f, side_p))


def units_of(rows, lanes):
    thirds = rows // 32 * 3 + jnp.minimum(3, (rows % 32 + 7) // 8)
    return jnp.where(lanes > 96, (rows + 7) // 8, jnp.where(lanes > 64, thirds, (rows + 15) // 16))


def kind_of(lanes):
    return jnp.where(lanes > 96, 0, jnp.where(lanes > 64, 1, 2))


def folded(kind, rows, lane_at):
    eight = [rows[k : k + 8] for k in range(0, CELL, 8)]
    out = []
    if kind == 1:
        for q in range(0, 16, 4):
            for u in range(3):
                moved = pltpu.roll(eight[q + 3], 96 - 32 * u, 1)
                out.append(jnp.where(lane_at[:8] < 96, eight[q + u], moved))
    else:
        for q in range(0, 8, 2):
            out.append(jnp.where(lane_at[:8] < 64, eight[q], pltpu.roll(eight[q + 1], 64, 1)))
    return jnp.concatenate(out, axis=0)


def unfolded(kind, rows, lane_at):
    eight = [rows[k : k + 8] for k in range(0, CELL, 8)]
    out = []
    if kind == 1:
        for q in range(0, 12, 3):
            out.extend(eight[q : q + 3])
            first, second, third = (pltpu.roll(eight[q + u], 32 * u + 32, 1) for u in range(3))
            out.append(jnp.where(lane_at[:8] < 32, first, jnp.where(lane_at[:8] < 64, second, third)))
    else:
        for q in range(4):
            out.extend((eight[q], pltpu.roll(eight[q], 64, 1)))
        out.extend(eight[8:])
    return jnp.concatenate(out, axis=0)


def tile_kernel(
    stage, first, second, live_a, live_b, own_f, own_p, *refs
):
    extra = (0, 3, 2)[stage]
    remote, refs = refs[:extra], refs[extra:]
    outs = (1, 2, 2)[stage]
    (w_a, w_b, radial, mix, out_w), refs = refs[:5], refs[5:]
    total, side = refs[0], refs[outs - 1]
    refs = refs[outs:]
    if stage == 0:
        given = (own_f, own_p, w_a, w_b, radial, mix, out_w)
        own_f, own_p, w_a, w_b, radial, mix, out_w = held = refs[-8:-1]
        copies = [pltpu.make_async_copy(*pair, refs[-1].at[k]) for k, pair in enumerate(zip(given, held))]
        for copy in copies:
            copy.start()
        for copy in copies:
            copy.wait()
        refs = refs[:-8]
    (
     flip, mix_t, mix_o, scale_o, last, onehot, proj_r, plain, dist, slope_sum, read_sum, proj_l, fb, pa, pb, near_rows, half_s, tilt_s, tiles, steps, kinds) = refs
    cells = own_f.shape[0] // CELL
    count = first.shape[0]

    flip[0] = jnp.transpose(w_a[...].astype(F32)).astype(BF)
    flip[1] = jnp.transpose(w_b[...].astype(F32)).astype(BF)
    mix_f = mix[...].astype(F32)
    mix_t[...] = (jnp.transpose(mix_f) * 0.5).astype(BF)
    mix_o[...] = (mix_f * 0.25).astype(BF)
    scale_o[...] = jnp.transpose(jnp.broadcast_to(out_w[...] / CELL, (CELL, CELL)))
    high = out_w[...].astype(BF)
    low = (out_w[...] - high.astype(F32)).astype(BF)
    pad = jnp.zeros((6, CELL), F32)
    left = jnp.concatenate([radial[...].astype(F32), jnp.zeros((8, CELL), F32)], axis=0)
    right = jnp.concatenate([jnp.zeros((NB, CELL), F32), high.astype(F32), low.astype(F32), pad], axis=0)
    last[...] = jnp.concatenate([left, right], axis=1).astype(BF)
    radial_h = radial[...].astype(F32) * 0.5
    row_of = lax.broadcasted_iota(jnp.int32, (2 * UNIT, UNIT * CELL), 0)
    at_lane = lax.broadcasted_iota(jnp.int32, (2 * UNIT, UNIT * CELL), 1)
    for kind, bound in enumerate((128, 96, 64)):
        held_row = at_lane // CELL + jnp.where(at_lane % CELL < bound, 0, UNIT)
        onehot[kind] = jnp.where(row_of == held_row, 1.0, 0.0).astype(BF)
    row_at = lax.broadcasted_iota(jnp.int32, (CELL, CELL), 0)
    lane_at = lax.broadcasted_iota(jnp.int32, (CELL, CELL), 1)
    centers = lax.broadcasted_iota(jnp.int32, (NB, CELL), 0).astype(F32) * (6.75 / NB)

    if stage == 0:
        total[...] = jnp.zeros_like(total)
    else:
        total[...] = remote[-1][...]
    if stage == 1:
        side[...] = jnp.zeros_like(side)

    picked, early = jnp.int32(0), jnp.int32(0)
    for t in range(count):
        block = second[t] // cells
        need = units_of(jnp.minimum(live_a[t], live_b[t]), jnp.maximum(live_a[t], live_b[t]))
        soon = (block == 0) & (early + need <= EARLY)
        early = early + jnp.where(soon, need, 0)
        take = (soon, (block < 2) & ~soon, block >= 2)[stage]
        tiles[picked] = jnp.int32(t)
        picked = picked + take.astype(jnp.int32)

    def prepare(s, so_far):
        t = tiles[s]
        cell = second[t] % cells
        pa[s] = tall(place_at(own_p, first[t]))
        if stage == 2:
            base = pl.multiple_of(t * PACKED, 16)
            fb[...] = remote[0][pl.ds(base, CELL), :]
            rest = remote[0][pl.ds(pl.multiple_of(base + CELL, 16), 16), :]
            pb[s] = rest.astype(F32)[0:8]
        else:
            def bring(feats, places):
                fb[...] = cell_at(feats, cell)
                pb[s] = tall(place_at(places, cell))

            if stage == 0:
                bring(own_f, own_p)
            else:
                pl.when(second[t] < cells)(functools.partial(bring, own_f, own_p))
                pl.when(second[t] >= cells)(functools.partial(bring, remote[0], remote[1]))
        num_a, num_b = live_a[t], live_b[t]
        swap = num_a > num_b
        feats_a, feats_b = cell_at(own_f, first[t]), fb[...]
        rows_f = jnp.where(swap, feats_b, feats_a)
        lanes_f = jnp.where(swap, feats_a, feats_b)
        rows_p, lanes_p = jnp.where(swap, pb[s], pa[s]), jnp.where(swap, pa[s], pb[s])
        w_r = jnp.where(swap, w_b[...], w_a[...])
        w_l = jnp.where(swap, flip[0], flip[1])
        proj_r[s] = dot(rows_f, w_r).astype(BF).astype(F32) * 0.5
        lane_proj = lax.dot_general(w_l, lanes_f, LAST, preferred_element_type=F32).astype(BF).astype(F32) * 0.5
        tall_p = jnp.transpose(rows_p)
        gaps = [tall_p[:, c : c + 1] - lanes_p[c : c + 1, :] for c in range(3)]
        r2 = gaps[0] * gaps[0] + gaps[1] * gaps[1] + gaps[2] * gaps[2]
        plain[s] = r2
        lanes = jnp.maximum(num_a, num_b)
        kind = kind_of(lanes)

        @pl.when(kind == 0)
        def _():
            dist[s] = r2
            proj_l[s, 0] = lane_proj

        @pl.when(kind == 1)
        def _():
            dist[s, 0:96, :] = folded(1, r2, lane_at)
            for u in range(3):
                proj_l[s, u] = jnp.where(lane_at < 96, lane_proj, pltpu.roll(lane_proj, 96 - 32 * u, 1))

        @pl.when(kind == 2)
        def _():
            dist[s, 0:32, :] = folded(2, r2, lane_at)
            proj_l[s, 0] = jnp.where(lane_at < 64, lane_proj, pltpu.roll(lane_proj, 64, 1))

        kinds[s] = kind
        n = units_of(jnp.minimum(num_a, num_b), lanes)
        steps[s] = n
        return so_far + n

    units = lax.fori_loop(0, picked, prepare, jnp.int32(0))

    proj_r[picked, 0:UNIT, :] = jnp.zeros((UNIT, CELL), F32)
    dist[picked, 0:UNIT, :] = jnp.zeros((UNIT, CELL), F32)
    kinds[picked] = jnp.int32(0)

    def after(s, g):
        over = g + 1 >= steps[s]
        return jnp.where(over, s + 1, s), jnp.where(over, 0, g + 1)

    def rows_of(ref, where):
        return [ref[s, pl.ds(pl.multiple_of(g * UNIT, UNIT), UNIT), :] for s, g in where]

    def enter(where):
        r2 = jnp.concatenate(rows_of(dist, where), axis=0)
        firsts, ones, lanes = [], [], []
        for k, (s, g) in enumerate(where):
            kind = kinds[s]
            third, part = g // 3, g % 3
            main = jnp.where(kind == 0, UNIT * g, jnp.where(kind == 1, 32 * third + UNIT * part, 2 * UNIT * g))
            more = jnp.where(kind == 0, UNIT * g, jnp.where(kind == 1, 32 * third + 3 * UNIT, 2 * UNIT * g + UNIT))
            for base in (main, more):
                firsts.append(proj_r[s, pl.ds(pl.multiple_of(base, UNIT), UNIT), :])
            blank = jnp.zeros((2 * UNIT, UNIT * CELL), BF)
            ones.append(jnp.concatenate([onehot[kind] if j == k else blank for j in range(UNITS)], axis=1))
            lanes.extend([proj_l[s, jnp.where(kind == 1, part, 0)]] * UNIT)
        weights = jnp.transpose(jnp.concatenate([radial_h, *firsts], axis=0)).astype(BF)
        offset = jnp.concatenate(
            [jnp.broadcast_to(r2[k : k + 1, :], (NB, CELL)) - centers for k in range(ROWS)], axis=1
        )
        basis = jnp.exp(-2.0 * offset * offset)
        inputs = jnp.concatenate([basis.astype(BF), *ones], axis=0)
        return r2, dot(weights, inputs) + jnp.concatenate(lanes, axis=1), basis * offset

    def rest(where, r2, half, tilt):
        bend = jnp.tanh(half)
        up = 1 + bend
        latent = half * up
        slope = up + latent * (1 - bend)
        pre = dot(mix_t[...], latent.astype(BF))
        bend = jnp.tanh(pre)
        up = 1 + bend
        act = pre * up
        near = 1.0 - r2 / 8.0
        near = near * near
        envelope = jnp.concatenate([near[k : k + 1, :] for k in range(ROWS)], axis=1)
        d_pre = envelope * jnp.concatenate([scale_o[...]] * ROWS, axis=1) * (up + act * (1 - bend))
        d_latent = dot(mix_o[...], d_pre.astype(BF))
        d_summed = (d_latent * slope).astype(BF)
        both = dot(last[...], jnp.concatenate([d_summed, act.astype(BF)], axis=0))
        d_r2 = jnp.sum(both[:NB] * tilt, axis=0, keepdims=True)
        readout = both[NB : NB + 1] + both[NB + 1 : NB + 2]
        for k, (s, g) in enumerate(where):
            cut = [slice(j * CELL, (j + 1) * CELL) for j in range(k * UNIT, (k + 1) * UNIT)]
            at = pl.ds(pl.multiple_of(g * UNIT, UNIT), UNIT)
            slope_sum[s, at, :] = jnp.concatenate([d_r2[:, c] for c in cut], axis=0)
            read_sum[s, at, :] = jnp.concatenate([readout[:, c] for c in cut], axis=0)

    def spread(s, g):
        where = [(s, g)]
        while len(where) < UNITS:
            s, g = after(*where[-1])
            where.append((jnp.minimum(s, picked), jnp.where(s < picked, g, 0)))
        return where

    last_tile = jnp.maximum(picked - 1, 0)

    def begin(where):
        r2, half_v, tilt_v = enter(where)
        near_rows[...] = r2
        half_s[...] = half_v
        tilt_s[...] = tilt_v

    def edges(_, here):
        where = spread(*here)
        r2, half_v, tilt_v = near_rows[...], half_s[...], tilt_s[...]
        s, g = after(*where[-1])
        nxt = spread(jnp.minimum(s, picked), jnp.where(s < picked, g, 0))
        rest(where, r2, half_v, tilt_v)
        begin(nxt)
        return nxt[0]

    begin(spread(jnp.int32(0), jnp.int32(0)))
    lax.fori_loop(0, (units + UNITS - 1) // UNITS, edges, (jnp.int32(0), jnp.int32(0)))

    def finish(s, _):
        t = tiles[s]
        num_a, num_b = live_a[t], live_b[t]
        swap = num_a > num_b
        rows_p, lanes_p = jnp.where(swap, pb[s], pa[s]), jnp.where(swap, pa[s], pb[s])
        live = (row_at < jnp.minimum(num_a, num_b)) & (lane_at < jnp.maximum(num_a, num_b))
        for kind in (1, 2):

            @pl.when(kinds[s] == kind)
            def _(kind=kind):
                slope_sum[s] = unfolded(kind, slope_sum[s], lane_at)
                read_sum[s] = unfolded(kind, read_sum[s], lane_at)

        near = 1.0 - plain[s] / 8.0
        pull = 2.0 * (-4.0 * slope_sum[s] - near * (0.25 / CELL) * read_sum[s])
        pull = jnp.where(live, pull, 0.0)
        high = pull.astype(BF)
        low = (pull - high.astype(F32)).astype(BF)

        def with_ones(places):
            rows = jnp.concatenate([places[0:3], jnp.ones((1, CELL), F32), jnp.zeros((4, CELL), F32)], axis=0)
            rows = rows.astype(BF)
            return jnp.concatenate([rows, rows], axis=1)

        over_lanes = lax.dot_general(
            with_ones(lanes_p), jnp.concatenate([high, low], axis=1), LAST, preferred_element_type=F32
        )
        over_rows = dot(with_ones(rows_p), jnp.concatenate([high, low], axis=0))
        grad_r = rows_p * over_lanes[3:4] - over_lanes
        grad_l = lanes_p * over_rows[3:4] - over_rows
        grad_a = jnp.where(swap, grad_l, grad_r)
        grad_b = jnp.where(swap, grad_r, grad_l)
        here = pl.ds(pl.multiple_of(first[t] * CELL, CELL), CELL)
        total[:, here] = total[:, here] + grad_a[0:3]
        there = pl.ds(pl.multiple_of(second[t] % cells * CELL, CELL), CELL)

        def add(sums):
            sums[:, there] = sums[:, there] + grad_b[0:3]

        if stage == 0:
            add(total)
        elif stage == 1:
            pl.when(second[t] < cells)(functools.partial(add, total))
            pl.when(second[t] >= cells)(functools.partial(add, side))
        else:
            side[t] = grad_b
        return 0

    lax.fori_loop(0, picked, finish, 0)


def hand_kernel(wanted, total, side, got, total_out, side_out):
    cells = total.shape[1] // CELL
    total_out[...] = total[...]
    side_out[...] = side[...]
    for slot in range(wanted.shape[0]):
        block = wanted[slot] // cells
        here = pl.ds(pl.multiple_of(wanted[slot] % cells * CELL, CELL), CELL)

        def add(sums, slot=slot, here=here):
            sums[:, here] = sums[:, here] + got[slot][0:3]

        pl.when(block == 2)(functools.partial(add, total_out))
        pl.when(block == 3)(functools.partial(add, side_out))


def last_kernel(total, got, out):
    out[...] = -(total[...] + got[...])


def called(kernel, prefetch, operands, out_shape, scratch=(), work=1.0, name=None, bring=False):
    if bring:
        scratch = [*scratch, *[pltpu.VMEM(x.shape, x.dtype) for x in operands]]
        scratch.append(pltpu.SemaphoreType.DMA((len(operands),)))
    return pl.pallas_call(
        kernel,
        grid_spec=pltpu.PrefetchScalarGridSpec(
            num_scalar_prefetch=len(prefetch),
            grid=(1,),
            in_specs=[pl.BlockSpec(memory_space=pltpu.HBM) if bring else VMEM] * len(operands),
            out_specs=jax.tree.map(lambda _: VMEM, out_shape),
            scratch_shapes=list(scratch),
        ),
        out_shape=out_shape,
        compiler_params=pltpu.CompilerParams(vmem_limit_bytes=(64000000 if bring else 40 << 20)),
        cost_estimate=pl.CostEstimate(flops=int(work * 1e9), bytes_accessed=1 << 20, transcendentals=0),
        name=name,
    )(*prefetch, *operands)


def on_device(
    positions,
    features,
    tile_first,
    tile_second,
    count_first,
    count_second,
    w_first,
    w_second,
    radial_weight,
    mix_weight,
    out_weight,
):
    slots = positions.shape[1]
    count = tile_first.shape[0]
    side_f = shifted(features, 0, 1)
    side_p = shifted(positions, 0, 1)
    asked = shifted(tile_second, -1, 0)

    scalars = (tile_first, tile_second, count_first, count_second)
    weights = (w_first, w_second, radial_weight, mix_weight, out_weight.reshape(1, -1))
    sums = jax.ShapeDtypeStruct((3, slots), F32)
    square = (count + 1, CELL, CELL)
    scratch = [
        pltpu.VMEM((2, CELL, CELL), BF),
        pltpu.VMEM((CELL, CELL), BF),
        pltpu.VMEM((CELL, CELL), BF),
        pltpu.VMEM((CELL, CELL), F32),
        pltpu.VMEM((24, 2 * CELL), BF),
        pltpu.VMEM((3, 2 * UNIT, UNIT * CELL), BF),
        *[pltpu.VMEM(square, F32)] * 5,
        pltpu.VMEM((count + 1, 3, CELL, CELL), F32),
        pltpu.VMEM((CELL, CELL), BF),
        *[pltpu.VMEM((count, 8, CELL), F32)] * 2,
        pltpu.VMEM((ROWS, CELL), F32),
        pltpu.VMEM((CELL, ROWS * CELL), F32),
        pltpu.VMEM((NB, ROWS * CELL), F32),
        *[pltpu.SMEM((count + 1,), jnp.int32)] * 3,
    ]

    def tiles(stage, extra, outs, work):
        operands = (features, positions, *extra, *weights)
        return called(
            functools.partial(tile_kernel, stage), scalars, operands, outs, scratch, work,
            f"tiles{stage}", bring=stage == 0,
        )

    (total,) = tiles(0, (), (sums,), 8.0)
    packed = called(
        pack_kernel,
        (asked,),
        (features, positions, side_f, side_p),
        jax.ShapeDtypeStruct((count * PACKED, CELL), BF),
        name="pack",
    )
    upper_cells = shifted(packed, 1, 0)
    total, side = tiles(1, (side_f, side_p, total), (sums, sums), 8.0)
    grads = jax.ShapeDtypeStruct((count, 8, CELL), F32)
    total, grads = tiles(2, (upper_cells, total), (sums, grads), 16.0)
    from_upper = shifted(grads, -1, 0)
    total, side = called(hand_kernel, (asked,), (total, side, from_upper), (sums, sums), name="hand")
    from_side = shifted(side, 0, -1)
    return called(last_kernel, (), (total, from_side), sums, name="last")


def solution(mesh):
    whole = ("grp", "dev")
    in_specs = (P(None, whole), P(whole, None), *[P(whole)] * 4, *[P()] * 5)
    return jax.shard_map(
        on_device, mesh=mesh, in_specs=in_specs, out_specs=P(None, whole), check_vma=False
    )
```

```python
import functools

import jax
import jax.numpy as jnp
from jax import lax
from jax.experimental import pallas as pl
from jax.experimental.pallas import tpu as pltpu
from jax.sharding import PartitionSpec as P

CELL = 128
NB = 16
UNIT = 8
UNITS = 2
ROWS = UNIT * UNITS
PACKED = CELL + 16
EARLY = 16
F32, BF = jnp.float32, jnp.bfloat16
LAST = (((1,), (1,)), ((), ()))
VMEM = pl.BlockSpec(memory_space=pltpu.VMEM)


def shifted(array, groups, members):
    n_grp, n_dev = lax.axis_size("grp"), lax.axis_size("dev")
    if groups == 0:
        return lax.ppermute(array, "dev", [(i, (i + members) % n_dev) for i in range(n_dev)])
    if members == 0:
        return lax.ppermute(array, "grp", [(i, (i + groups) % n_grp) for i in range(n_grp)])
    pairs = [
        (g * n_dev + d, (g + groups) % n_grp * n_dev + (d + members) % n_dev)
        for g in range(n_grp)
        for d in range(n_dev)
    ]
    return lax.ppermute(array, ("grp", "dev"), pairs)


def dot(a, b):
    return jnp.dot(a, b, preferred_element_type=F32)


def cell_at(ref, cell):
    return ref[pl.ds(pl.multiple_of(cell * CELL, CELL), CELL), :]


def place_at(ref, cell):
    return ref[:, pl.ds(pl.multiple_of(cell * CELL, CELL), CELL)]


def tall(places):
    return jnp.concatenate([places.astype(F32), jnp.zeros((5, CELL), F32)], axis=0)


def pack_kernel(wanted, own_f, own_p, side_f, side_p, out):
    cells = own_f.shape[0] // CELL
    for slot in range(wanted.shape[0]):
        block, cell = wanted[slot] // cells, wanted[slot] % cells

        def put(feats, places, slot=slot, cell=cell):
            base = slot * PACKED
            out[base : base + CELL, :] = cell_at(feats, cell)
            rows = jnp.concatenate([tall(place_at(places, cell)), jnp.zeros((8, CELL), F32)], axis=0)
            out[base + CELL : base + PACKED, :] = rows.astype(BF)

        pl.when(block == 2)(functools.partial(put, own_f, own_p))
        pl.when(block == 3)(functools.partial(put, side_f, side_p))


LANES = (128, 96, 64)
PARTS = (1, 3, 1)


def kind_of(lanes):
    return sum((lanes <= bound).astype(jnp.int32) for bound in LANES[1:])


def units_of(rows, lanes):
    blocks = lax.shift_right_logical(rows + 7, 3)
    units = blocks
    for bound, parts in zip(LANES[1:], PARTS[1:]):
        whole = lax.shift_right_logical(blocks, {1: 1, 3: 2}[parts])
        shared = whole * parts + jnp.minimum(parts, blocks - whole * (parts + 1))
        units = jnp.where(lanes <= bound, shared, units)
    return units


def turned(a, b):
    return units_of(b, a) < units_of(a, b)


def folded(kind, rows, lane_at):
    eight = [rows[k : k + 8] for k in range(0, CELL, 8)]
    bound, parts = LANES[kind], PARTS[kind]
    out = []
    for q in range(0, 16, parts + 1):
        for u in range(parts):
            moved = pltpu.roll(eight[q + parts], (bound - (CELL - bound) * u) % CELL, 1)
            out.append(jnp.where(lane_at[:8] < bound, eight[q + u], moved))
    return jnp.concatenate(out, axis=0)


def unfolded(kind, rows, lane_at):
    eight = [rows[k : k + 8] for k in range(0, CELL, 8)]
    parts, width = PARTS[kind], CELL - LANES[kind]
    out = []
    for q in range(0, 16 // (parts + 1) * parts, parts):
        out.extend(eight[q : q + parts])
        block = None
        for u in range(parts):
            moved = pltpu.roll(eight[q + u], width * (u + 1) % CELL, 1)
            block = moved if u == 0 else jnp.where(lane_at[:8] < width * u, block, moved)
        out.append(block)
    return jnp.concatenate(out, axis=0)


def tile_kernel(
    stage, first, second, live_a, live_b, own_f, own_p, *refs
):
    extra = (0, 3, 2)[stage]
    remote, refs = refs[:extra], refs[extra:]
    outs = (1, 2, 2)[stage]
    (w_a, w_b, radial, mix, out_w), refs = refs[:5], refs[5:]
    total, side = refs[0], refs[outs - 1]
    refs = refs[outs:]
    if stage == 0:
        given = (own_f, own_p, w_a, w_b, radial, mix, out_w)
        own_f, own_p, w_a, w_b, radial, mix, out_w = held = refs[-8:-1]
        copies = [pltpu.make_async_copy(*pair, refs[-1].at[k]) for k, pair in enumerate(zip(given, held))]
        for copy in copies:
            copy.start()
        for copy in copies:
            copy.wait()
        refs = refs[:-8]
    (
     flip, mix_t, mix_o, scale_o, last, onehot, proj_r, plain, dist, slope_sum, read_sum, proj_l, fb, pa, pb, near_rows, half_s, tilt_s, tiles, steps, kinds, flips) = refs
    cells = own_f.shape[0] // CELL
    count = first.shape[0]

    flip[0] = jnp.transpose(w_a[...].astype(F32)).astype(BF)
    flip[1] = jnp.transpose(w_b[...].astype(F32)).astype(BF)
    mix_f = mix[...].astype(F32)
    mix_t[...] = (jnp.transpose(mix_f) * 0.5).astype(BF)
    mix_o[...] = (mix_f * 0.25).astype(BF)
    scale_o[...] = jnp.transpose(jnp.broadcast_to(out_w[...] / CELL, (CELL, CELL)))
    high = out_w[...].astype(BF)
    low = (out_w[...] - high.astype(F32)).astype(BF)
    pad = jnp.zeros((6, CELL), F32)
    left = jnp.concatenate([radial[...].astype(F32), jnp.zeros((8, CELL), F32)], axis=0)
    right = jnp.concatenate([jnp.zeros((NB, CELL), F32), high.astype(F32), low.astype(F32), pad], axis=0)
    last[...] = jnp.concatenate([left, right], axis=1).astype(BF)
    radial_h = radial[...].astype(F32) * 0.5
    row_of = lax.broadcasted_iota(jnp.int32, (2 * UNIT, UNIT * CELL), 0)
    at_lane = lax.broadcasted_iota(jnp.int32, (2 * UNIT, UNIT * CELL), 1)
    for kind, bound in enumerate(LANES):
        held_row = at_lane // CELL + jnp.where(at_lane % CELL < bound, 0, UNIT)
        onehot[kind] = jnp.where(row_of == held_row, 1.0, 0.0).astype(BF)
    row_at = lax.broadcasted_iota(jnp.int32, (CELL, CELL), 0)
    lane_at = lax.broadcasted_iota(jnp.int32, (CELL, CELL), 1)
    centers = lax.broadcasted_iota(jnp.int32, (NB, CELL), 0).astype(F32) * (6.75 / NB)

    if stage == 0:
        total[...] = jnp.zeros_like(total)
    else:
        total[...] = remote[-1][...]
    if stage == 1:
        side[...] = jnp.zeros_like(side)

    picked, early = jnp.int32(0), jnp.int32(0)
    for t in range(count):
        block = lax.div(second[t], cells)
        need = jnp.minimum(units_of(live_a[t], live_b[t]), units_of(live_b[t], live_a[t]))
        soon = (block == 0) & (early + need <= EARLY)
        early = early + jnp.where(soon, need, 0)
        take = (soon, (block < 2) & ~soon, block >= 2)[stage]
        tiles[picked] = jnp.int32(t)
        picked = picked + take.astype(jnp.int32)

    def prepare(s, so_far):
        t = tiles[s]
        cell = lax.rem(second[t], cells)
        pa[s] = tall(place_at(own_p, first[t]))
        if stage == 2:
            base = pl.multiple_of(t * PACKED, 16)
            fb[...] = remote[0][pl.ds(base, CELL), :]
            rest = remote[0][pl.ds(pl.multiple_of(base + CELL, 16), 16), :]
            pb[s] = rest.astype(F32)[0:8]
        else:
            def bring(feats, places):
                fb[...] = cell_at(feats, cell)
                pb[s] = tall(place_at(places, cell))

            if stage == 0:
                bring(own_f, own_p)
            else:
                pl.when(second[t] < cells)(functools.partial(bring, own_f, own_p))
                pl.when(second[t] >= cells)(functools.partial(bring, remote[0], remote[1]))
        num_a, num_b = live_a[t], live_b[t]
        swap = turned(num_a, num_b)
        feats_a, feats_b = cell_at(own_f, first[t]), fb[...]
        rows_f = jnp.where(swap, feats_b, feats_a)
        lanes_f = jnp.where(swap, feats_a, feats_b)
        rows_p, lanes_p = jnp.where(swap, pb[s], pa[s]), jnp.where(swap, pa[s], pb[s])
        w_r = jnp.where(swap, w_b[...], w_a[...])
        w_l = jnp.where(swap, flip[0], flip[1])
        proj_r[s] = dot(rows_f, w_r).astype(BF).astype(F32) * 0.5
        lane_proj = lax.dot_general(w_l, lanes_f, LAST, preferred_element_type=F32).astype(BF).astype(F32) * 0.5
        tall_p = jnp.transpose(rows_p)
        gaps = [tall_p[:, c : c + 1] - lanes_p[c : c + 1, :] for c in range(3)]
        r2 = gaps[0] * gaps[0] + gaps[1] * gaps[1] + gaps[2] * gaps[2]
        plain[s] = r2
        rows, lanes = jnp.where(swap, num_b, num_a), jnp.where(swap, num_a, num_b)
        kind = kind_of(lanes)
        proj_l[s, 0] = lane_proj
        dist[s] = r2
        for fold in range(1, len(LANES)):

            @pl.when(kind == fold)
            def _(fold=fold):
                bound, parts = LANES[fold], PARTS[fold]
                dist[s, 0 : CELL // (parts + 1) * parts, :] = folded(fold, r2, lane_at)
                for u in range(parts):
                    moved = pltpu.roll(lane_proj, (bound - (CELL - bound) * u) % CELL, 1)
                    proj_l[s, u] = jnp.where(lane_at < bound, lane_proj, moved)

        kinds[s] = kind
        flips[s] = swap.astype(jnp.int32)
        n = units_of(rows, lanes)
        steps[s] = n
        return so_far + n

    units = lax.fori_loop(0, picked, prepare, jnp.int32(0))

    proj_r[picked, 0:UNIT, :] = jnp.zeros((UNIT, CELL), F32)
    dist[picked, 0:UNIT, :] = jnp.zeros((UNIT, CELL), F32)
    kinds[picked] = jnp.int32(0)

    def after(s, g):
        over = g + 1 >= steps[s]
        return jnp.where(over, s + 1, s), jnp.where(over, 0, g + 1)

    def rows_of(ref, where):
        return [ref[s, pl.ds(pl.multiple_of(g * UNIT, UNIT), UNIT), :] for s, g in where]

    def enter(where):
        r2 = jnp.concatenate(rows_of(dist, where), axis=0)
        firsts, ones, lanes = [], [], []
        for k, (s, g) in enumerate(where):
            kind = kinds[s]
            main, more, part = UNIT * g, UNIT * g, jnp.int32(0)
            for fold in range(1, len(LANES)):
                parts = PARTS[fold]
                turn = lax.div(g, parts) if parts > 1 else g
                place = g - turn * parts
                group = UNIT * (parts + 1) * turn
                main = jnp.where(kind == fold, group + UNIT * place, main)
                more = jnp.where(kind == fold, group + UNIT * parts, more)
                part = jnp.where(kind == fold, place, part)
            for base in (main, more):
                firsts.append(proj_r[s, pl.ds(pl.multiple_of(base, UNIT), UNIT), :])
            blank = jnp.zeros((2 * UNIT, UNIT * CELL), BF)
            ones.append(jnp.concatenate([onehot[kind] if j == k else blank for j in range(UNITS)], axis=1))
            lanes.extend([proj_l[s, part]] * UNIT)
        weights = jnp.transpose(jnp.concatenate([radial_h, *firsts], axis=0)).astype(BF)
        offset = jnp.concatenate(
            [jnp.broadcast_to(r2[k : k + 1, :], (NB, CELL)) - centers for k in range(ROWS)], axis=1
        )
        basis = jnp.exp(-2.0 * offset * offset)
        inputs = jnp.concatenate([basis.astype(BF), *ones], axis=0)
        return r2, dot(weights, inputs) + jnp.concatenate(lanes, axis=1), basis * offset

    def rest(where, r2, half, tilt):
        bend = jnp.tanh(half)
        up = 1 + bend
        latent = half * up
        slope = up + latent * (1 - bend)
        pre = dot(mix_t[...], latent.astype(BF))
        bend = jnp.tanh(pre)
        up = 1 + bend
        act = pre * up
        near = 1.0 - r2 / 8.0
        near = near * near
        envelope = jnp.concatenate([near[k : k + 1, :] for k in range(ROWS)], axis=1)
        d_pre = envelope * jnp.concatenate([scale_o[...]] * ROWS, axis=1) * (up + act * (1 - bend))
        d_latent = dot(mix_o[...], d_pre.astype(BF))
        d_summed = (d_latent * slope).astype(BF)
        both = dot(last[...], jnp.concatenate([d_summed, act.astype(BF)], axis=0))
        d_r2 = jnp.sum(both[:NB] * tilt, axis=0, keepdims=True)
        readout = both[NB : NB + 1] + both[NB + 1 : NB + 2]
        for k, (s, g) in enumerate(where):
            cut = [slice(j * CELL, (j + 1) * CELL) for j in range(k * UNIT, (k + 1) * UNIT)]
            at = pl.ds(pl.multiple_of(g * UNIT, UNIT), UNIT)
            slope_sum[s, at, :] = jnp.concatenate([d_r2[:, c] for c in cut], axis=0)
            read_sum[s, at, :] = jnp.concatenate([readout[:, c] for c in cut], axis=0)

    def spread(s, g):
        where = [(s, g)]
        while len(where) < UNITS:
            s, g = after(*where[-1])
            where.append((jnp.minimum(s, picked), jnp.where(s < picked, g, 0)))
        return where

    last_tile = jnp.maximum(picked - 1, 0)

    def begin(where):
        r2, half_v, tilt_v = enter(where)
        near_rows[...] = r2
        half_s[...] = half_v
        tilt_s[...] = tilt_v

    def edges(_, here):
        where = spread(*here)
        r2, half_v, tilt_v = near_rows[...], half_s[...], tilt_s[...]
        s, g = after(*where[-1])
        nxt = spread(jnp.minimum(s, picked), jnp.where(s < picked, g, 0))
        rest(where, r2, half_v, tilt_v)
        begin(nxt)
        return nxt[0]

    begin(spread(jnp.int32(0), jnp.int32(0)))
    lax.fori_loop(0, (units + UNITS - 1) // UNITS, edges, (jnp.int32(0), jnp.int32(0)))

    def finish(s, _):
        t = tiles[s]
        num_a, num_b = live_a[t], live_b[t]
        swap = flips[s] == 1
        rows_p, lanes_p = jnp.where(swap, pb[s], pa[s]), jnp.where(swap, pa[s], pb[s])
        live = (row_at < jnp.where(swap, num_b, num_a)) & (lane_at < jnp.where(swap, num_a, num_b))
        for kind in range(1, len(LANES)):

            @pl.when(kinds[s] == kind)
            def _(kind=kind):
                slope_sum[s] = unfolded(kind, slope_sum[s], lane_at)
                read_sum[s] = unfolded(kind, read_sum[s], lane_at)

        near = 1.0 - plain[s] / 8.0
        pull = 2.0 * (-4.0 * slope_sum[s] - near * (0.25 / CELL) * read_sum[s])
        pull = jnp.where(live, pull, 0.0)
        high = pull.astype(BF)
        low = (pull - high.astype(F32)).astype(BF)

        def with_ones(places):
            rows = jnp.concatenate([places[0:3], jnp.ones((1, CELL), F32), jnp.zeros((4, CELL), F32)], axis=0)
            rows = rows.astype(BF)
            return jnp.concatenate([rows, rows], axis=1)

        over_lanes = lax.dot_general(
            with_ones(lanes_p), jnp.concatenate([high, low], axis=1), LAST, preferred_element_type=F32
        )
        over_rows = dot(with_ones(rows_p), jnp.concatenate([high, low], axis=0))
        grad_r = rows_p * over_lanes[3:4] - over_lanes
        grad_l = lanes_p * over_rows[3:4] - over_rows
        grad_a = jnp.where(swap, grad_l, grad_r)
        grad_b = jnp.where(swap, grad_r, grad_l)
        here = pl.ds(pl.multiple_of(first[t] * CELL, CELL), CELL)
        total[:, here] = total[:, here] + grad_a[0:3]
        there = pl.ds(pl.multiple_of(lax.rem(second[t], cells) * CELL, CELL), CELL)

        def add(sums):
            sums[:, there] = sums[:, there] + grad_b[0:3]

        if stage == 0:
            add(total)
        elif stage == 1:
            pl.when(second[t] < cells)(functools.partial(add, total))
            pl.when(second[t] >= cells)(functools.partial(add, side))
        else:
            side[t] = grad_b
        return 0

    lax.fori_loop(0, picked, finish, 0)


def hand_kernel(wanted, total, side, got, total_out, side_out):
    cells = total.shape[1] // CELL
    total_out[...] = total[...]
    side_out[...] = side[...]
    for slot in range(wanted.shape[0]):
        block = wanted[slot] // cells
        here = pl.ds(pl.multiple_of(wanted[slot] % cells * CELL, CELL), CELL)

        def add(sums, slot=slot, here=here):
            sums[:, here] = sums[:, here] + got[slot][0:3]

        pl.when(block == 2)(functools.partial(add, total_out))
        pl.when(block == 3)(functools.partial(add, side_out))


def last_kernel(total, got, out):
    out[...] = -(total[...] + got[...])


def called(kernel, prefetch, operands, out_shape, scratch=(), work=1.0, name=None, bring=False):
    if bring:
        scratch = [*scratch, *[pltpu.VMEM(x.shape, x.dtype) for x in operands]]
        scratch.append(pltpu.SemaphoreType.DMA((len(operands),)))
    return pl.pallas_call(
        kernel,
        grid_spec=pltpu.PrefetchScalarGridSpec(
            num_scalar_prefetch=len(prefetch),
            grid=(1,),
            in_specs=[pl.BlockSpec(memory_space=pltpu.HBM) if bring else VMEM] * len(operands),
            out_specs=jax.tree.map(lambda _: VMEM, out_shape),
            scratch_shapes=list(scratch),
        ),
        out_shape=out_shape,
        compiler_params=pltpu.CompilerParams(vmem_limit_bytes=(64000000 if bring else 40 << 20)),
        cost_estimate=pl.CostEstimate(flops=int(work * 1e9), bytes_accessed=1 << 20, transcendentals=0),
        name=name,
    )(*prefetch, *operands)


def on_device(
    positions,
    features,
    tile_first,
    tile_second,
    count_first,
    count_second,
    w_first,
    w_second,
    radial_weight,
    mix_weight,
    out_weight,
):
    slots = positions.shape[1]
    count = tile_first.shape[0]
    side_f = shifted(features, 0, 1)
    side_p = shifted(positions, 0, 1)
    asked = shifted(tile_second, -1, 0)

    scalars = (tile_first, tile_second, count_first, count_second)
    weights = (w_first, w_second, radial_weight, mix_weight, out_weight.reshape(1, -1))
    sums = jax.ShapeDtypeStruct((3, slots), F32)
    square = (count + 1, CELL, CELL)
    scratch = [
        pltpu.VMEM((2, CELL, CELL), BF),
        pltpu.VMEM((CELL, CELL), BF),
        pltpu.VMEM((CELL, CELL), BF),
        pltpu.VMEM((CELL, CELL), F32),
        pltpu.VMEM((24, 2 * CELL), BF),
        pltpu.VMEM((len(LANES), 2 * UNIT, UNIT * CELL), BF),
        *[pltpu.VMEM(square, F32)] * 5,
        pltpu.VMEM((count + 1, max(PARTS), CELL, CELL), F32),
        pltpu.VMEM((CELL, CELL), BF),
        *[pltpu.VMEM((count, 8, CELL), F32)] * 2,
        pltpu.VMEM((ROWS, CELL), F32),
        pltpu.VMEM((CELL, ROWS * CELL), F32),
        pltpu.VMEM((NB, ROWS * CELL), F32),
        *[pltpu.SMEM((count + 1,), jnp.int32)] * 4,
    ]

    def tiles(stage, extra, outs, work):
        operands = (features, positions, *extra, *weights)
        return called(
            functools.partial(tile_kernel, stage), scalars, operands, outs, scratch, work,
            f"tiles{stage}", bring=stage == 0,
        )

    (total,) = tiles(0, (), (sums,), 8.0)
    packed = called(
        pack_kernel,
        (asked,),
        (features, positions, side_f, side_p),
        jax.ShapeDtypeStruct((count * PACKED, CELL), BF),
        name="pack",
    )
    upper_cells = shifted(packed, 1, 0)
    total, side = tiles(1, (side_f, side_p, total), (sums, sums), 8.0)
    grads = jax.ShapeDtypeStruct((count, 8, CELL), F32)
    total, grads = tiles(2, (upper_cells, total), (sums, grads), 16.0)
    from_upper = shifted(grads, -1, 0)
    total, side = called(hand_kernel, (asked,), (total, side, from_upper), (sums, sums), name="hand")
    from_side = shifted(side, 0, -1)
    return called(last_kernel, (), (total, from_side), sums, name="last")


def solution(mesh):
    whole = ("grp", "dev")
    in_specs = (P(None, whole), P(whole, None), *[P(whole)] * 4, *[P()] * 5)
    return jax.shard_map(
        on_device, mesh=mesh, in_specs=in_specs, out_specs=P(None, whole), check_vma=False
    )
```
